32 devices in a mesh: section: 2 (over core), shard: 4 (over y, x), replica: 4 (over z).
Axes of the slice: x: 2, y: 2, z: 4, core: 2. Of those that a mesh axis runs over, the one named last changes fastest.
Arguments:
- inputs: bfloat16 [8, 256, 960], P('replica', 'shard'), may hold values from -6 to 6
- cotangent: bfloat16 [8, 256, 960], P('replica', 'shard'), may hold values from -6 to 6
- segments: int32 [8, 256], P('replica'), may hold values from 0 to 3, never falling along the last dimension, each value on 1 to 128 neighbouring positions
- attn_q: bfloat16 [2, 960, 960], P('section', None, 'shard'), may hold values from -0.1875 to 0.1875
- attn_k: bfloat16 [2, 960, 320], P('section', None, 'shard'), may hold values from -0.1875 to 0.1875
- attn_v: bfloat16 [2, 960, 320], P('section', None, 'shard'), may hold values from -0.1875 to 0.1875
- attn_out: bfloat16 [2, 960, 960], P('section', None, 'shard'), may hold values from -0.75 to 0.75
- ffn_gate: bfloat16 [2, 960, 2560], P('section', None, 'shard'), may hold values from -0.1875 to 0.1875
- ffn_up: bfloat16 [2, 960, 2560], P('section', None, 'shard'), may hold values from -0.1875 to 0.1875
- ffn_down: bfloat16 [2, 2560, 960], P('section', 'shard'), may hold values from -0.125 to 0.125
- norm_gains: float32 [2, 2, 960], P('section'), may hold values from 0.1 to 1.9
Outputs:
- activations: bfloat16 [2, 8, 256, 960], P('section', 'replica', 'shard')
- input_grads: bfloat16 [2, 8, 256, 960], P('section', 'replica', 'shard')
- grad_q: float32 [2, 960, 960], P('section', 'replica', 'shard')
- grad_k: float32 [2, 960, 320], P('section', 'replica', 'shard')
- grad_v: float32 [2, 960, 320], P('section', 'replica', 'shard')
- grad_out: float32 [2, 960, 960], P('section', 'replica', 'shard')
- grad_gate: float32 [2, 960, 2560], P('section', 'replica', 'shard')
- grad_up: float32 [2, 960, 2560], P('section', 'replica', 'shard')
- grad_down: float32 [2, 2560, 960], P('section', 'shard', 'replica')
- grad_gains: float32 [2, 2, 960], P('section')
The draws below stay inside these ranges and needn't reach their ends.
Inputs may be any that keep to these rules, and one draw needn't show every extreme that they name: `segments`: segment numbers never fall along a row, and every one of the 4 numbers occurs in every row.
All inputs are finite; a program needn't handle non-finite values.
Results may differ from the reference program's by a relative error of at most 0.024.
Values may be sent and summed in bfloat16 or wider, within the bound.
No kernel may reach another device: no remote copies, remote signals or barrier semaphores. Data moves between devices by JAX's collectives and lax.ppermute only.
A program may use at most 128 MiB of HBM per device.

```python
import math
import jax
import jax.numpy as jnp
import numpy as np
from jax import lax

D = 960
HQ = 15
KV = 5
HD = 64
FF = 2560
SEQ = 256
MICRO = 2
DOCS = 4
ROWS = 8


def block_levels(key, shape, cuts, smallest, high):
    gain, own = 1.0, jax.random.fold_in(key, 6)
    for dim, shards_of in cuts:
        steps = jnp.exp(jax.random.uniform(jax.random.fold_in(own, dim), (shards_of,), jnp.float32, smallest / len(cuts), high / len(cuts)))
        gain = gain * jnp.repeat(steps, shape[dim] // shards_of).reshape([-1 if axis == dim else 1 for axis in range(len(shape))])
    return gain


def length_profile(count, total, bound, slope):
    weights = [(1 << 20) // math.isqrt(standing ** slope) + 1 for standing in range(2, count + 1)]
    surplus, given = total - bound - (count - 1), [1] * (count - 1)
    while surplus > 0:
        movable = [i for i in range(count - 1) if given[i] < bound]
        pool, budget = sum([weights[i] for i in movable]), surplus
        for i in movable:
            more = min(bound - given[i], max(1, budget * weights[i] // pool), surplus)
            given[i] = given[i] + more
            surplus = surplus - more
    return np.array([bound] + given)


def ragged_sizes(key, number_of, total, most, skew):
    if number_of == 2:
        one = jax.random.randint(key, (), max(1, total - most), min(most, total - 1) + 1)
        return jnp.stack([one, total - one])
    lengths = jnp.asarray(length_profile(number_of, total, most, skew), jnp.int32)
    twos = (number_of - 1) // 2
    giver, sink = lengths[1:1 + 2 * twos:2], lengths[2:2 + 2 * twos:2]
    room = jnp.minimum(giver - 1, most - sink)
    passed = jax.random.randint(jax.random.fold_in(key, 1), (twos,), 0, 1 << 20) % (room + 1)
    lengths = lengths.at[1:1 + 2 * twos:2].set(giver - passed).at[2:2 + 2 * twos:2].set(sink + passed)
    return lengths[jax.random.permutation(jax.random.fold_in(key, 2), number_of)]


def scatter_about(own_key, extent, scale, reach, split=(), kind=jnp.bfloat16):
    array = scale * jax.random.normal(own_key, extent, jnp.float32)
    if split:
        array = array * block_levels(own_key, extent, split, -0.22, 0.18)
    return jnp.clip(array, -reach, reach).astype(kind)


def setup_inputs(seed: int = 0) -> dict:
    key_list = jax.random.split(jax.random.key(seed), 12)
    return {
        "inputs": scatter_about(key_list[0], (ROWS, SEQ, D), 1.0, 6.0, ((0, 4), (1, 4))),
        "cotangent": scatter_about(key_list[1], (ROWS, SEQ, D), 1.0, 6.0, ((0, 4), (1, 4))),
        "segments": jax.vmap(lambda own: jnp.searchsorted(jnp.cumsum(ragged_sizes(own, DOCS, SEQ, SEQ // 2, 1)), jnp.arange(SEQ), side="right"))(jax.random.split(key_list[2], ROWS)).reshape((ROWS, SEQ)).astype(jnp.int32),
        "attn_q": scatter_about(key_list[3], (2, D, HQ * HD), D ** -0.5, 0.1875, ((0, 2), (2, 4))),
        "attn_k": scatter_about(key_list[4], (2, D, KV * HD), D ** -0.5, 0.1875, ((0, 2), (2, 4))),
        "attn_v": scatter_about(key_list[5], (2, D, KV * HD), D ** -0.5, 0.1875, ((0, 2), (2, 4))),
        "attn_out": scatter_about(key_list[6], (2, HQ * HD, D), (HQ * HD // 16) ** -0.5, 0.75, ((0, 2), (2, 4))),
        "ffn_gate": scatter_about(key_list[7], (2, D, FF), D ** -0.5, 0.1875, ((0, 2), (2, 4))),
        "ffn_up": scatter_about(key_list[8], (2, D, FF), D ** -0.5, 0.1875, ((0, 2), (2, 4))),
        "ffn_down": scatter_about(key_list[9], (2, FF, D), FF ** -0.5, 0.125, ((0, 2), (1, 4))),
        "norm_gains": jnp.clip(1.0 + 0.18 * jax.random.normal(key_list[10], (2, 2, D), jnp.float32), 0.1, 1.9),
    }


epsilon = 1e-05
rope_base = 10000.0
masked_score = -1e+30

def matmul(left, right):
    return jnp.dot(left, right, preferred_element_type=jnp.float32)

def rope_tables(segments):
    length = segments.shape[-1]
    position = jnp.arange(length, dtype=jnp.int32)
    before = jnp.concatenate([segments[:, :1] - 1, segments[:, :-1]], axis=1)
    starts = jnp.where(segments != before, position, 0).astype(jnp.int32)
    starts = lax.cummax(starts, axis=1)
    places = (position - starts).astype(jnp.float32)
    frequency = rope_base ** (jnp.arange(HD // 2, dtype=jnp.float32) * (-2.0 / HD))
    angles = places[..., None] * frequency
    return (jnp.cos(angles), jnp.sin(angles))

def allowed_mask(segments):
    length = segments.shape[-1]
    position = jnp.arange(length, dtype=jnp.int32)
    same_doc = segments[:, :, None] == segments[:, None, :]
    return same_doc & (position[:, None] >= position[None, :])[None]

def rotate(values, cosine, sine_table):
    half_dim = values.shape[-1] // 2
    first_half = values[..., :half_dim]
    second_half = values[..., half_dim:]
    return jnp.concatenate([first_half * cosine - second_half * sine_table, second_half * cosine + first_half * sine_table], axis=-1)

def rotate_back(cotang, cosine, sine_table):
    half_dim = cotang.shape[-1] // 2
    first_half = cotang[..., :half_dim]
    second_half = cotang[..., half_dim:]
    return jnp.concatenate([first_half * cosine + second_half * sine_table, second_half * cosine - first_half * sine_table], axis=-1)

def score_block(queries, key_rows, allowed):
    scores = jnp.einsum('gqkrd,gpkd->gkrqp', queries.astype(jnp.float32), key_rows.astype(jnp.float32)) * HD ** (-0.5)
    return jnp.where(allowed[:, None, None], scores, masked_score)

def attend_forward(queries, key_rows, value_rows, allowed):
    scores = score_block(queries, key_rows, allowed)
    row_max = lax.optimization_barrier(jnp.max(scores, axis=-1, keepdims=True))
    log_total = row_max + jnp.log(lax.optimization_barrier(jnp.sum(jnp.exp(scores - row_max), axis=-1, keepdims=True)))
    prob_rows = jnp.exp(scores - log_total).astype(jnp.bfloat16)
    attended = jnp.einsum('gkrqp,gpkd->gqkrd', prob_rows.astype(jnp.float32), value_rows.astype(jnp.float32))
    return (log_total, attended.astype(jnp.bfloat16))

def attend_backward(queries, key_rows, value_rows, allowed, log_total, attended, d_attended):
    scores = score_block(queries, key_rows, allowed)
    prob_full = jnp.exp(scores - log_total)
    prob_rows = prob_full.astype(jnp.bfloat16)
    d_probs = jnp.einsum('gqkrd,gpkd->gkrqp', d_attended.astype(jnp.float32), value_rows.astype(jnp.float32))
    delta = jnp.einsum('gqkrd,gqkrd->gkrq', d_attended.astype(jnp.float32), attended.astype(jnp.float32))
    d_scores = (prob_full * (d_probs - delta[..., None]) * HD ** (-0.5)).astype(jnp.bfloat16)
    d_queries = jnp.einsum('gkrqp,gpkd->gqkrd', d_scores.astype(jnp.float32), key_rows.astype(jnp.float32))
    d_keys = jnp.einsum('gkrqp,gqkrd->gpkd', d_scores.astype(jnp.float32), queries.astype(jnp.float32))
    d_values = jnp.einsum('gkrqp,gqkrd->gpkd', prob_rows.astype(jnp.float32), d_attended.astype(jnp.float32))
    return (d_queries, d_keys, d_values)

def layer_forward(layer_in, segments, weights):
    weight_q, weight_k, weight_v, weight_out, weight_gate, weight_up, weight_down, gain_attn, gain_ffn = weights
    groups, length = segments.shape
    tokens_all = groups * length
    group_size = HQ // KV
    cosine, sine_table = rope_tables(segments)
    cosine = cosine[:, :, None, :]
    sine_table = sine_table[:, :, None, :]
    allowed = allowed_mask(segments)
    inputs_f = layer_in.reshape(tokens_all, D).astype(jnp.float32)
    inv_attn = lax.rsqrt(lax.optimization_barrier(jnp.mean(inputs_f * inputs_f, axis=-1, keepdims=True)) + epsilon)
    normed = (inputs_f * inv_attn * gain_attn).astype(jnp.bfloat16)
    queries = rotate(matmul(normed, weight_q).reshape(groups, length, HQ, HD), cosine, sine_table).astype(jnp.bfloat16)
    queries = queries.reshape(groups, length, KV, group_size, HD)
    key_rows = rotate(matmul(normed, weight_k).reshape(groups, length, KV, HD), cosine, sine_table).astype(jnp.bfloat16)
    value_rows = matmul(normed, weight_v).astype(jnp.bfloat16).reshape(groups, length, KV, HD)
    log_total, attended = attend_forward(queries, key_rows, value_rows, allowed)
    attended_flat = attended.reshape(tokens_all, HQ * HD)
    middle = inputs_f + matmul(attended_flat, weight_out)
    inv_ffn = lax.rsqrt(lax.optimization_barrier(jnp.mean(middle * middle, axis=-1, keepdims=True)) + epsilon)
    normed_ffn = (middle * inv_ffn * gain_ffn).astype(jnp.bfloat16)
    gate_pre = matmul(normed_ffn, weight_gate)
    up_pre = matmul(normed_ffn, weight_up)
    hidden = (jax.nn.silu(gate_pre) * up_pre).astype(jnp.bfloat16)
    layer_out = (middle + matmul(hidden, weight_down)).astype(jnp.bfloat16)
    saved = (inputs_f, inv_attn, normed, queries, key_rows, value_rows, log_total, attended, middle, inv_ffn, normed_ffn, gate_pre, up_pre, hidden)
    return (layer_out.reshape(groups, length, D), saved)

def layer_backward(upstream_in, segments, weights, saved):
    weight_q, weight_k, weight_v, weight_out, weight_gate, weight_up, weight_down, gain_attn, gain_ffn = weights
    inputs_f, inv_attn, normed, queries, key_rows, value_rows, log_total, attended, middle, inv_ffn, normed_ffn, gate_pre, up_pre, hidden = saved
    groups, length = segments.shape
    tokens_all = groups * length
    group_size = HQ // KV
    cosine, sine_table = rope_tables(segments)
    cosine = cosine[:, :, None, :]
    sine_table = sine_table[:, :, None, :]
    allowed = allowed_mask(segments)
    upstream = upstream_in.reshape(tokens_all, D)
    d_hidden = matmul(upstream, weight_down.T)
    sigma = jax.nn.sigmoid(gate_pre)
    d_gate = (d_hidden * up_pre * sigma * (1.0 + gate_pre * (1.0 - sigma))).astype(jnp.bfloat16)
    d_up = (d_hidden * gate_pre * sigma).astype(jnp.bfloat16)
    d_normed_ffn = matmul(d_gate, weight_gate.T) + matmul(d_up, weight_up.T)
    scaled_ffn = d_normed_ffn * gain_ffn
    d_middle = upstream.astype(jnp.float32) + inv_ffn * scaled_ffn - middle * (inv_ffn * inv_ffn * inv_ffn) * lax.optimization_barrier(jnp.mean(scaled_ffn * middle, axis=-1, keepdims=True))
    d_middle_b = d_middle.astype(jnp.bfloat16)
    d_attended = matmul(d_middle_b, weight_out.T).astype(jnp.bfloat16).reshape(groups, length, KV, group_size, HD)
    d_queries, d_keys, d_values = attend_backward(queries, key_rows, value_rows, allowed, log_total, attended, d_attended)
    d_q_rot = rotate_back(d_queries.reshape(groups, length, HQ, HD), cosine, sine_table).reshape(tokens_all, HQ * HD).astype(jnp.bfloat16)
    d_k_rot = rotate_back(d_keys, cosine, sine_table).reshape(tokens_all, KV * HD).astype(jnp.bfloat16)
    d_v_rows = d_values.reshape(tokens_all, KV * HD).astype(jnp.bfloat16)
    d_normed = matmul(d_q_rot, weight_q.T) + matmul(d_k_rot, weight_k.T) + matmul(d_v_rows, weight_v.T)
    scaled_attn = d_normed * gain_attn
    d_inputs = d_middle + inv_attn * scaled_attn - inputs_f * (inv_attn * inv_attn * inv_attn) * lax.optimization_barrier(jnp.mean(scaled_attn * inputs_f, axis=-1, keepdims=True))
    d_inputs = d_inputs.astype(jnp.bfloat16).reshape(groups, length, D)
    attended_flat = attended.reshape(tokens_all, HQ * HD)
    gain_terms = jnp.stack([lax.optimization_barrier(jnp.sum(d_normed * inputs_f * inv_attn, axis=0)), lax.optimization_barrier(jnp.sum(d_normed_ffn * middle * inv_ffn, axis=0))])
    grads = (matmul(normed.T, d_q_rot), matmul(normed.T, d_k_rot), matmul(normed.T, d_v_rows), matmul(attended_flat.T, d_middle_b), matmul(normed_ffn.T, d_gate), matmul(normed_ffn.T, d_up), matmul(hidden.T, upstream), gain_terms)
    return (d_inputs, grads)

def rounded_group(grads):
    return tuple(grads)

def zero_grads():
    return (jnp.zeros((D, HQ * HD), jnp.float32), jnp.zeros((D, KV * HD), jnp.float32), jnp.zeros((D, KV * HD), jnp.float32), jnp.zeros((HQ * HD, D), jnp.float32), jnp.zeros((D, FF), jnp.float32), jnp.zeros((D, FF), jnp.float32), jnp.zeros((FF, D), jnp.float32), jnp.zeros((2, D), jnp.float32))

def reference(inputs, cotangent, segments, attn_q, attn_k, attn_v, attn_out, ffn_gate, ffn_up, ffn_down, norm_gains):
    block_count = ROWS // MICRO
    layer_one = (attn_q[0], attn_k[0], attn_v[0], attn_out[0], ffn_gate[0], ffn_up[0], ffn_down[0], norm_gains[0, 0], norm_gains[0, 1])
    layer_two = (attn_q[1], attn_k[1], attn_v[1], attn_out[1], ffn_gate[1], ffn_up[1], ffn_down[1], norm_gains[1, 0], norm_gains[1, 1])

    def one_block(running, block_in):
        x_block, cot_block, seg_block = block_in
        middle_acts, saved_one = layer_forward(x_block, seg_block, layer_one)
        final_acts, saved_two = layer_forward(middle_acts, seg_block, layer_two)
        d_middle_acts, grads_two = layer_backward(cot_block, seg_block, layer_two, saved_two)
        d_first, grads_one = layer_backward(d_middle_acts, seg_block, layer_one, saved_one)
        addition = (rounded_group(grads_one), rounded_group(grads_two))
        running = jax.tree.map(lambda before_sum, addend: before_sum + addend, running, addition)
        return (running, (middle_acts, final_acts, d_first, d_middle_acts))
    blocks = (inputs.reshape(block_count, MICRO, SEQ, D), cotangent.reshape(block_count, MICRO, SEQ, D), segments.reshape(block_count, MICRO, SEQ))
    totals, stacked = lax.scan(one_block, (zero_grads(), zero_grads()), blocks)
    activations = jnp.stack([stacked[0].reshape(ROWS, SEQ, D), stacked[1].reshape(ROWS, SEQ, D)])
    input_grads = jnp.stack([stacked[2].reshape(ROWS, SEQ, D), stacked[3].reshape(ROWS, SEQ, D)])
    outputs = [jnp.stack([totals[0][slot], totals[1][slot]]) for slot in range(8)]
    return (activations, input_grads, outputs[0], outputs[1], outputs[2], outputs[3], outputs[4], outputs[5], outputs[6], outputs[7])
```

```python
import jax
import jax.numpy as jnp
from jax import lax
from jax.sharding import PartitionSpec as P

HQ = 15
KV = 5
HD = 64
GROUP = HQ // KV

epsilon = 1e-05
rope_base = 10000.0
masked_score = -1e30

BF = jnp.bfloat16
F32 = jnp.float32


def dot(left, right, left_dim, right_dim):
    return lax.dot_general(
        left, right, (((left_dim,), (right_dim,)), ((), ())), preferred_element_type=F32
    )


def swap(block, axis, bit):
    return lax.ppermute(block, axis, [(i, i ^ bit) for i in range(lax.axis_size(axis))])


def shard_sum(part):
    half = part.shape[0] // 2
    a, b = part[:half], part[half:]
    a_in, b_in = swap(a, "shard", 1), swap(b, "shard", 2)
    a = (a.astype(F32) + a_in.astype(F32)).astype(BF)
    b = (b.astype(F32) + b_in.astype(F32)).astype(BF)
    a_in, b_in = swap(a, "shard", 2), swap(b, "shard", 1)
    return jnp.concatenate(
        [a.astype(F32) + a_in.astype(F32), b.astype(F32) + b_in.astype(F32)], axis=0
    )


def shard_scatter(part, shard_at):
    rows = part.shape[0] // 4

    def block(at):
        return lax.dynamic_slice_in_dim(part, at * rows, rows, 0)

    total = block(shard_at).astype(F32)
    for bit in (1, 2, 3):
        total = total + swap(block(shard_at ^ bit), "shard", bit).astype(F32)
    return total


def shard_blocks(own):
    half = own.shape[0] // 2
    one, two = swap(own, "shard", 1), swap(own, "shard", 2)
    top, bottom = swap(one[:half], "shard", 2), swap(two[half:], "shard", 1)
    return [own, one, two, jnp.concatenate([top, bottom], axis=0)]


def shard_gather(own, shard_at):
    rows = own.shape[0]
    out = jnp.zeros((4 * rows,) + own.shape[1:], own.dtype)
    for bit, block in enumerate(shard_blocks(own)):
        out = lax.dynamic_update_slice_in_dim(out, block, (shard_at ^ bit) * rows, 0)
    return out


def line_scatter(chunks, axis):
    n = lax.axis_size(axis)
    if n > 8:
        return lax.psum_scatter(chunks.astype(F32), axis, scatter_dimension=0, tiled=False)
    at = lax.axis_index(axis)
    right = [(i, i + 1) for i in range(n - 1)]
    left = [(i + 1, i) for i in range(n - 1)]

    def pick(index):
        return lax.dynamic_index_in_dim(chunks, jnp.clip(index, 0, n - 1), 0, keepdims=False)

    from_left = from_right = None
    for step in range(n - 1):
        to_right = pick(n - 1 - step + at)
        to_left = pick(step - (n - 1 - at))
        if step:
            to_right = (to_right.astype(F32) + from_left.astype(F32)).astype(BF)
            to_left = (to_left.astype(F32) + from_right.astype(F32)).astype(BF)
        from_left = lax.ppermute(to_right, axis, right)
        from_right = lax.ppermute(to_left, axis, left)
    return pick(at).astype(F32) + from_left.astype(F32) + from_right.astype(F32)


def line_sum(block, axis):
    bit = 1
    while bit < lax.axis_size(axis):
        block = block + swap(block, axis, bit)
        bit *= 2
    return block


def rope_tables(segments):
    length = segments.shape[-1]
    position = jnp.arange(length, dtype=jnp.int32)
    before = jnp.concatenate([segments[:1] - 1, segments[:-1]])
    starts = jnp.where(segments != before, position, 0)
    starts = jnp.max(
        jnp.where(position[None, :] <= position[:, None], starts[None, :], 0), axis=1
    )
    places = (position - starts).astype(F32)
    frequency = rope_base ** (jnp.arange(HD // 2, dtype=F32) * (-2.0 / HD))
    angles = places[:, None] * frequency
    return (jnp.cos(angles)[:, None, :], jnp.sin(angles)[:, None, :])


def rotate(values, cosine, sine_table):
    first, second = values[..., : HD // 2], values[..., HD // 2 :]
    return jnp.concatenate(
        [first * cosine - second * sine_table, second * cosine + first * sine_table], axis=-1
    )


def scores_of(queries, keys, allowed):
    scores = jnp.einsum("qkrd,pkd->krqp", queries, keys, preferred_element_type=F32) * HD ** (-0.5)
    return jnp.where(allowed[None, None], scores, masked_score)


def attention_block(x, weights, gain, tables):
    cosine, sine_table, allowed = tables
    length = x.shape[0]
    x_f = x.astype(F32)
    inv = lax.rsqrt(jnp.mean(x_f * x_f, axis=-1, keepdims=True) + epsilon)
    normed = (x_f * inv * gain).astype(BF)
    weight_q, weight_k, weight_v, weight_o = weights
    queries = rotate(dot(normed, weight_q, 1, 1).reshape(length, HQ, HD), cosine, sine_table)
    queries = queries.astype(BF).reshape(length, KV, GROUP, HD)
    keys = rotate(dot(normed, weight_k, 1, 1).reshape(length, KV, HD), cosine, sine_table)
    keys = keys.astype(BF)
    values = dot(normed, weight_v, 1, 1).astype(BF).reshape(length, KV, HD)
    scores = scores_of(queries, keys, allowed)
    row_max = jnp.max(scores, axis=-1, keepdims=True)
    log_total = row_max + jnp.log(jnp.sum(jnp.exp(scores - row_max), axis=-1, keepdims=True))
    probs = jnp.exp(scores - log_total).astype(BF)
    attended = jnp.einsum("krqp,pkd->qkrd", probs, values, preferred_element_type=F32).astype(BF)
    middle = x_f + dot(attended.reshape(length, HQ * HD), weight_o, 1, 1)
    return middle, (x_f, inv, normed, queries, keys, values, log_total, attended)


def ffn_block(middle, gain, weight_gate, weight_up, weight_down):
    inv = lax.rsqrt(jnp.mean(middle * middle, axis=-1, keepdims=True) + epsilon)
    normed = (middle * inv * gain).astype(BF)
    gate_pre = dot(normed, weight_gate, 1, 0)
    up_pre = dot(normed, weight_up, 1, 0)
    hidden = (jax.nn.silu(gate_pre) * up_pre).astype(BF)
    part = dot(hidden, weight_down, 1, 0).astype(BF)
    return part, (middle, inv, normed, gate_pre, up_pre, hidden)


def ffn_backward(upstream, saved, weight_gate, weight_up, weight_down):
    _, _, _, gate_pre, up_pre, _ = saved
    d_hidden = dot(upstream, weight_down, 1, 1)
    sigma = jax.nn.sigmoid(gate_pre)
    d_gate = (d_hidden * up_pre * sigma * (1.0 + gate_pre * (1.0 - sigma))).astype(BF)
    d_up = (d_hidden * gate_pre * sigma).astype(BF)
    part = (dot(d_gate, weight_gate, 1, 1) + dot(d_up, weight_up, 1, 1)).astype(BF)
    return part, d_gate, d_up


def norm_backward(upstream, d_normed, x, inv, gain):
    scaled = d_normed * gain
    return (
        upstream
        + inv * scaled
        - x * (inv * inv * inv) * jnp.mean(scaled * x, axis=-1, keepdims=True)
    )


def attention_backward(d_middle_b, saved, weights, tables):
    cosine, sine_table, allowed = tables
    _, _, _, queries, keys, values, log_total, attended = saved
    weight_q, weight_k, weight_v, weight_o = weights
    length = d_middle_b.shape[0]
    d_attended = dot(d_middle_b, weight_o, 1, 0).astype(BF).reshape(length, KV, GROUP, HD)
    prob_full = jnp.exp(scores_of(queries, keys, allowed) - log_total)
    d_probs = jnp.einsum("qkrd,pkd->krqp", d_attended, values, preferred_element_type=F32)
    delta = jnp.einsum("qkrd,qkrd->krq", d_attended, attended, preferred_element_type=F32)
    d_scores = (prob_full * (d_probs - delta[..., None]) * HD ** (-0.5)).astype(BF)
    d_q = jnp.einsum("krqp,pkd->qkrd", d_scores, keys, preferred_element_type=F32)
    d_k = jnp.einsum("krqp,qkrd->pkd", d_scores, queries, preferred_element_type=F32)
    d_v = jnp.einsum(
        "krqp,qkrd->pkd", prob_full.astype(BF), d_attended, preferred_element_type=F32
    )
    d_q = rotate(d_q.reshape(length, HQ, HD), cosine, -sine_table).astype(BF)
    d_k = rotate(d_k, cosine, -sine_table).astype(BF)
    d_q = d_q.reshape(length, HQ * HD)
    d_k = d_k.reshape(length, KV * HD)
    d_v = d_v.astype(BF).reshape(length, KV * HD)
    d_normed = dot(d_q, weight_q, 1, 0) + dot(d_k, weight_k, 1, 0) + dot(d_v, weight_v, 1, 0)
    return d_normed, d_q, d_k, d_v


def local(
    inputs,
    cotangent,
    segments,
    attn_q,
    attn_k,
    attn_v,
    attn_out,
    ffn_gate,
    ffn_up,
    ffn_down,
    norm_gains,
):
    core = lax.axis_index("section")
    shard_at = lax.axis_index("shard")
    first = core == 0
    block_len = inputs.shape[1]
    replicas = lax.axis_size("replica")

    def partner(block):
        return swap(block, "section", 1)

    def pick(zero, one):
        return jnp.where(first, zero, one)

    def both_layers(own):
        other = partner(own)
        return pick(own, other), pick(other, own)

    def mine(stacked):
        return lax.dynamic_index_in_dim(stacked, core, 0, keepdims=False)

    q_cols, kv_cols = attn_q.shape[2], attn_k.shape[2]
    o_cols = attn_out.shape[2]

    def gathered(own, rows):
        half = rows // 2
        got = partner(pick(own[half:], own[:half]))
        zero = pick(own[:half], got)
        one = pick(got, own[half:])
        layers = []
        for mine_half in (zero, one):
            blocks = jnp.stack(shard_blocks(mine_half))
            blocks_other = partner(blocks)
            full = jnp.concatenate(
                [pick(blocks, blocks_other), pick(blocks_other, blocks)], axis=1
            )
            layers.append([full[shard_at ^ at] for at in range(4)])
        return layers

    qkv_own = jnp.concatenate([attn_q[0], attn_k[0], attn_v[0]], axis=1).T
    qkv_layers = gathered(qkv_own, q_cols + 2 * kv_cols)
    out_layers = gathered(attn_out[0].T, o_cols)
    attn_weights = []
    for layer in range(2):
        pieces = qkv_layers[layer]
        attn_weights.append(
            (
                jnp.concatenate([piece[:q_cols] for piece in pieces], axis=0),
                jnp.concatenate([piece[q_cols : q_cols + kv_cols] for piece in pieces], axis=0),
                jnp.concatenate([piece[q_cols + kv_cols :] for piece in pieces], axis=0),
                jnp.concatenate(out_layers[layer], axis=0),
            )
        )
    gate_layers = both_layers(ffn_gate[0])
    up_layers = both_layers(ffn_up[0])
    down_layers = both_layers(ffn_down[0])
    gain_layers = both_layers(norm_gains[0])

    seg = mine(segments)
    length = seg.shape[0]
    position = jnp.arange(length, dtype=jnp.int32)
    allowed = (seg[:, None] == seg[None, :]) & (position[:, None] >= position[None, :])
    tables = rope_tables(seg) + (allowed,)

    x = shard_gather(mine(inputs), shard_at)
    upstream = shard_gather(mine(cotangent), shard_at)

    def own_rows(full):
        return lax.dynamic_slice_in_dim(full, shard_at * block_len, block_len, 0)

    attn_saved, ffn_saved, own_out = [], [], []
    for layer in range(2):
        gain = gain_layers[layer]
        middle, saved = attention_block(x, attn_weights[layer], gain[0], tables)
        attn_saved.append(saved)
        part, saved = ffn_block(
            middle, gain[1], gate_layers[layer], up_layers[layer], down_layers[layer]
        )
        ffn_saved.append(saved)
        if layer == 0:
            x = (middle + shard_sum(part)).astype(BF)
            own_out.append(own_rows(x))
        else:
            own_out.append((own_rows(middle) + shard_scatter(part, shard_at)).astype(BF))

    def token_pair(block):
        return jnp.concatenate([block, partner(block)], axis=0)

    def half_pair(block):
        half = block.shape[1] // 2
        keep = pick(block[:, :half], block[:, half:])
        send = pick(block[:, half:], block[:, :half])
        return jnp.concatenate([keep, partner(send)], axis=0)

    def kind_pair(zero, one):
        return jnp.concatenate([pick(zero, one), partner(pick(one, zero))], axis=0)

    def row_chunks(grad):
        rows = grad.shape[0] // replicas
        return grad.astype(BF).reshape(replicas, rows, grad.shape[1])

    def own_cols(block, cols):
        return lax.dynamic_slice_in_dim(block, shard_at * cols, cols, 1)

    own_grads, gains_out, reduced = [None, None], [None, None], [None, None]
    for layer in (1, 0):
        gain = gain_layers[layer]
        middle, inv_f, normed_f, _, _, hidden = ffn_saved[layer]
        part, d_gate, d_up = ffn_backward(
            upstream,
            ffn_saved[layer],
            gate_layers[layer],
            up_layers[layer],
            down_layers[layer],
        )
        normed_pair = token_pair(normed_f)
        grad_gate_up = dot(
            normed_pair, jnp.concatenate([half_pair(d_gate), half_pair(d_up)], axis=1), 0, 0
        )
        grad_down = dot(token_pair(upstream), half_pair(hidden), 0, 0)
        ffn_reduced = line_scatter(
            row_chunks(jnp.concatenate([grad_gate_up, grad_down], axis=1)), "replica"
        )
        d_normed_ffn = shard_sum(part)
        d_middle = norm_backward(upstream.astype(F32), d_normed_ffn, middle, inv_f, gain[1])
        d_middle_b = d_middle.astype(BF)
        saved = attn_saved[layer]
        d_normed, d_q, d_k, d_v = attention_backward(
            d_middle_b, saved, attn_weights[layer], tables
        )
        x_f, inv_a, normed_a = saved[:3]
        attended = saved[7].reshape(length, HQ * HD)
        upstream = norm_backward(d_middle, d_normed, x_f, inv_a, gain[0]).astype(BF)
        own_grads[layer] = own_rows(upstream)
        grad_qo = dot(
            kind_pair(normed_a, attended),
            kind_pair(own_cols(d_q, q_cols), own_cols(d_middle_b, o_cols)),
            0,
            0,
        )
        grad_kv = dot(
            token_pair(normed_a),
            kind_pair(own_cols(d_k, kv_cols), own_cols(d_v, kv_cols)),
            0,
            0,
        )
        attn_reduced = line_scatter(
            row_chunks(jnp.concatenate([grad_qo, grad_kv], axis=1)), "replica"
        )
        reduced[layer] = jnp.concatenate([ffn_reduced, attn_reduced], axis=1)
        gains_out[layer] = jnp.stack(
            [
                jnp.sum(d_normed * x_f * inv_a, axis=0),
                jnp.sum(d_normed_ffn * middle * inv_f, axis=0),
            ]
        )

    def to_owner(zero, one):
        got = partner(pick(one, zero))
        return pick(zero, got), pick(got, one)

    acts = jnp.stack(to_owner(own_out[0], own_out[1]))
    grads = jnp.stack(to_owner(own_grads[0], own_grads[1]))
    lo, hi = to_owner(reduced[0], reduced[1])
    half = ffn_gate.shape[2] // 2

    def halves(start):
        return jnp.concatenate([lo[:, start : start + half], hi[:, start : start + half]], axis=1)

    final_gate, final_up = halves(0), halves(half)
    final_down = halves(2 * half).T
    base = 3 * half
    final_q = lo[:, base : base + q_cols]
    final_out = hi[:, base : base + o_cols]
    final_k = lo[:, base + q_cols :]
    final_v = hi[:, base + o_cols :]
    gain_parts = to_owner(gains_out[0], gains_out[1])
    gains_total = line_sum(gain_parts[0] + gain_parts[1], "replica")
    return (
        acts[None],
        grads[None],
        final_q[None],
        final_k[None],
        final_v[None],
        final_out[None],
        final_gate[None],
        final_up[None],
        final_down[None],
        gains_total[None],
    )


def solution(mesh):
    placed = (
        P("replica", "shard", None),
        P("replica", "shard", None),
        P("replica", None),
        P("section", None, "shard"),
        P("section", None, "shard"),
        P("section", None, "shard"),
        P("section", None, "shard"),
        P("section", None, "shard"),
        P("section", None, "shard"),
        P("section", "shard", None),
        P("section", None, None),
    )
    return jax.shard_map(
        local,
        mesh=mesh,
        in_specs=placed,
        out_specs=(
            P("section", "replica", "shard", None),
            P("section", "replica", "shard", None),
            P("section", "replica", "shard"),
            P("section", "replica", "shard"),
            P("section", "replica", "shard"),
            P("section", "replica", "shard"),
            P("section", "replica", "shard"),
            P("section", "replica", "shard"),
            P("section", "shard", "replica"),
            P("section", None, None),
        ),
        check_vma=False,
    )
```

```python
import functools

import jax
import jax.numpy as jnp
from jax import lax
from jax.experimental import pallas as pl
from jax.experimental.pallas import tpu as pltpu
from jax.sharding import PartitionSpec as P

HQ = 15
KV = 5
HD = 64
GROUP = HQ // KV

epsilon = 1e-05
rope_base = 10000.0
masked_score = -1e30
scale = HD**-0.5

BF = jnp.bfloat16
F32 = jnp.float32


def dot(left, right, left_dim, right_dim):
    return lax.dot_general(
        left, right, (((left_dim,), (right_dim,)), ((), ())), preferred_element_type=F32
    )


def shape(dims, dtype):
    return jax.ShapeDtypeStruct(dims, dtype)


def call(body, name, arrays, outs, scratch=(), in_hbm=()):
    specs = [pl.BlockSpec(memory_space=pltpu.SMEM)] + [
        pl.BlockSpec(memory_space=pl.ANY if at in in_hbm else pltpu.VMEM)
        for at in range(1, len(arrays))
    ]
    return pl.pallas_call(
        body,
        name=name,
        in_specs=specs,
        out_specs=[pl.BlockSpec(memory_space=pltpu.VMEM) for _ in outs],
        out_shape=list(outs),
        scratch_shapes=list(scratch),
        compiler_params=pltpu.CompilerParams(vmem_limit_bytes=60 * 1024 * 1024),
    )(*arrays)


class Copies:
    def __init__(self, sems):
        self.sems, self.plain, self.cond = sems, [], []
        self.used = 0

    def _make(self, source, target):
        sem = self.sems.at[self.used]
        self.used += 1
        return pltpu.make_async_copy(source, target, sem)

    def add(self, source, target):
        copy = self._make(source, target)
        copy.start()
        self.plain.append(copy)

    def add_when(self, cond, pairs):
        made = [self._make(source, target) for source, target in pairs]

        @pl.when(cond)
        def _():
            for copy in made:
                copy.start()

        self.cond.append((cond, made))

    def wait(self):
        for copy in self.plain:
            copy.wait()
        for cond, made in self.cond:

            @pl.when(cond)
            def _(made=made):
                for copy in made:
                    copy.wait()


def start_qkv(place, sources, target, sems, q_cols, kv_cols):
    core, shard_at = place[0], place[1]
    own, one, two, half, half_other = sources
    cols = q_cols + 2 * kv_cols
    low = (cols // 2 + 15) // 16 * 16
    kv_rows = 4 * kv_cols
    copies = Copies(sems)
    pieces = ((0, q_cols, 0), (q_cols, kv_cols, 4 * q_cols), (q_cols + kv_cols, kv_cols, 4 * q_cols + kv_rows))

    def rows(block, source, first, last, source_first):
        out = []
        for start, size, base in pieces:
            lo, hi = max(start, first), min(start + size, last)
            if lo < hi:
                at = pl.multiple_of(base + block * size + (lo - start), 16)
                out.append(
                    (
                        source.at[pl.ds(lo - source_first, hi - lo)],
                        target.at[pl.ds(at, hi - lo)],
                    )
                )
        return out

    for block, source in (
        (shard_at, own),
        (shard_at ^ (1 + core), one),
        (shard_at ^ (2 - core), two),
    ):
        for pair in rows(block, source, 0, cols, 0):
            copies.add(*pair)
    across = shard_at ^ 3
    for at in range(2):
        top, bottom = (half, half_other) if at == 0 else (half_other, half)
        copies.add_when(
            core == at,
            rows(across, top, 0, low, 0) + rows(across, bottom, low, cols, cols - low),
        )
    return copies


def start_out(place, sources, target, sems, cols):
    core, shard_at = place[0], place[1]
    own, one, two, half, half_other = sources
    low = (cols // 2 + 15) // 16 * 16
    copies = Copies(sems)

    def at_row(block, offset):
        return pl.multiple_of(block * cols + offset, 16)

    for block, source in (
        (shard_at, own),
        (shard_at ^ (1 + core), one),
        (shard_at ^ (2 - core), two),
    ):
        copies.add(source, target.at[pl.ds(at_row(block, 0), cols)])
    across = shard_at ^ 3
    rest = cols - low
    for at in range(2):
        top, bottom = (half, half_other) if at == 0 else (half_other, half)
        copies.add_when(
            core == at,
            [
                (top, target.at[pl.ds(at_row(across, 0), low)]),
                (
                    bottom.at[pl.ds(low - rest, rest)],
                    target.at[pl.ds(at_row(across, low), rest)],
                ),
            ],
        )
    return copies


def start_ffn(place, layer, sources, targets, sems):
    copies = Copies(sems)
    for (own, other), target in zip(sources, targets):
        copies.add_when(place[0] == layer, [(own, target)])
        copies.add_when(place[0] != layer, [(other, target)])
    return copies


def turn_rows(values, cosine, sine_table, heads):
    half = HD // 2
    out = []
    for head in range(heads):
        a = values[head * HD : head * HD + half]
        b = values[head * HD + half : (head + 1) * HD]
        out.append(a * cosine - b * sine_table)
        out.append(b * cosine + a * sine_table)
    return jnp.concatenate(out, axis=0)


def allowed_rows(seg_col, seg_row):
    length = seg_col.shape[0]
    key_at = lax.broadcasted_iota(jnp.int32, (length, length), 0)
    query_at = lax.broadcasted_iota(jnp.int32, (length, length), 1)
    return (seg_col == seg_row) & (key_at <= query_at)


def inverse_rms(values):
    return lax.rsqrt(jnp.mean(values * values, axis=-1, keepdims=True) + epsilon)


def forward_body(layer, widths, place, *refs):
    refs = list(refs)

    def take(count):
        out = refs[:count]
        del refs[:count]
        return out

    q_cols, kv_cols, o_cols = widths
    if layer:
        before, a, a_in, b, b_in = take(5)
    else:
        (x_ref,) = take(1)
    qkv_sources, out_sources = take(5), take(5)
    ffn_sources = [take(2) for _ in range(3)]
    gain, cosine_ref, sine_ref, seg_col, seg_row = take(5)
    if layer:
        (x_out,) = take(1)
    normed_t, q_t, k_t, v_t, lse, att_t, middle_out, normed_f_out, gate_out, up_out, hidden_out = take(11)
    parts = take(1 if layer else 2)
    w_qkv, w_out, w_gate, w_up, w_down, qkv_sems, out_sems, ffn_sems = take(8)

    qkv_copies = start_qkv(place, qkv_sources, w_qkv, qkv_sems, q_cols, kv_cols)
    out_copies = start_out(place, out_sources, w_out, out_sems, o_cols)
    ffn_copies = start_ffn(place, layer, ffn_sources, (w_gate, w_up, w_down), ffn_sems)

    if layer:
        half = a.shape[0]
        x_out[:half] = (before[:half] + (a[...].astype(F32) + a_in[...].astype(F32))).astype(BF)
        x_out[half:] = (before[half:] + (b[...].astype(F32) + b_in[...].astype(F32))).astype(BF)
        x = x_out[...].astype(F32)
    else:
        x = x_ref[...].astype(F32)
    normed = (x * inverse_rms(x) * gain[0:1]).astype(BF)
    normed_t[...] = normed.T
    cosine, sine_table = cosine_ref[...], sine_ref[...]
    allowed = allowed_rows(seg_col[...], seg_row[...])
    qkv_copies.wait()
    q_rows, kv_rows = HQ * HD, KV * HD
    qkv = dot(w_qkv[...], normed, 1, 1)
    q_t[...] = turn_rows(qkv[:q_rows], cosine, sine_table, HQ).astype(BF)
    k_t[...] = turn_rows(qkv[q_rows : q_rows + kv_rows], cosine, sine_table, KV).astype(BF)
    v_t[...] = qkv[q_rows + kv_rows :].astype(BF)
    lse[...] = jnp.zeros(lse.shape, F32)
    for head in range(HQ):
        key = (head // GROUP) * HD
        scores = dot(k_t[key : key + HD], q_t[head * HD : (head + 1) * HD], 0, 0) * scale
        scores = jnp.where(allowed, scores, masked_score)
        top = jnp.max(scores, axis=0, keepdims=True)
        weight = jnp.exp(scores - top)
        total = jnp.sum(weight, axis=0, keepdims=True)
        lse[head : head + 1] = top + jnp.log(total)
        probs = (weight * (1.0 / total)).astype(BF)
        att_t[head * HD : (head + 1) * HD] = dot(v_t[key : key + HD], probs, 1, 0).astype(BF)
    out_copies.wait()
    middle = x + dot(att_t[...].T, w_out[...], 1, 1)
    middle_out[...] = middle
    normed_f = (middle * inverse_rms(middle) * gain[1:2]).astype(BF)
    normed_f_out[...] = normed_f
    ffn_copies.wait()
    gate_pre = dot(normed_f, w_gate[...], 1, 0)
    up_pre = dot(normed_f, w_up[...], 1, 0)
    gate_out[...] = gate_pre
    up_out[...] = up_pre
    hidden = (gate_pre / (1.0 + jnp.exp(-gate_pre)) * up_pre).astype(BF)
    hidden_out[...] = hidden
    part = dot(hidden, w_down[...], 1, 0).astype(BF)
    if layer:
        parts[0][...] = part
    else:
        half = part.shape[0] // 2
        parts[0][...] = part[:half]
        parts[1][...] = part[half:]


def ffn_backward_body(layer, place, upstream_ref, gate_ref, up_ref, hidden_ref, normed_ref, *refs):
    sources = [refs[0:2], refs[2:4], refs[4:6]]
    send, keep, part_a, part_b, w_gate, w_up, w_down, sems = refs[6:]
    copies = start_ffn(place, layer, sources, (w_gate, w_up, w_down), sems)
    upstream, gate_pre, up_pre = upstream_ref[...], gate_ref[...], up_ref[...]
    send[1] = normed_ref[...]
    send[2] = upstream
    copies.wait()
    d_hidden = dot(upstream, w_down[...], 1, 1)
    sigma = 1.0 / (1.0 + jnp.exp(-gate_pre))
    d_gate = (d_hidden * up_pre * sigma * (1.0 + gate_pre * (1.0 - sigma))).astype(BF)
    d_up = (d_hidden * gate_pre * sigma).astype(BF)
    part = (dot(d_gate, w_gate[...], 1, 1) + dot(d_up, w_up[...], 1, 1)).astype(BF)
    half = part.shape[0] // 2
    part_a[...] = part[:half]
    part_b[...] = part[half:]
    wide = d_gate.shape[1] // 2
    blocks = (d_gate, d_up, hidden_ref[...])
    low = jnp.concatenate([block[:, :wide] for block in blocks], axis=1)
    high = jnp.concatenate([block[:, wide:] for block in blocks], axis=1)
    is_low = place[0] == 0

    @pl.when(is_low)
    def _():
        keep[...] = low
        send[0] = high

    @pl.when(jnp.logical_not(is_low))
    def _():
        keep[...] = high
        send[0] = low


def ffn_grad_body(place, keep, normed, upstream, got, out):
    chunks, rows, wide = out.shape
    two_thirds = wide * 2 // 3
    first = dot(normed[...], keep[:, :two_thirds], 0, 0) + dot(got[1], got[0, :, :two_thirds], 0, 0)
    second = dot(upstream[...], keep[:, two_thirds:], 0, 0) + dot(
        got[2], got[0, :, two_thirds:], 0, 0
    )
    both = jnp.concatenate([first, second], axis=1).astype(BF)
    for chunk in range(chunks):
        out[chunk] = both[chunk * rows : (chunk + 1) * rows]


def attention_backward_body(widths, place, *refs):
    refs = list(refs)

    def take(count):
        out = refs[:count]
        del refs[:count]
        return out

    q_cols, kv_cols, o_cols = widths
    a, a_in, b, b_in, upstream_ref, middle_ref, x_ref = take(7)
    normed_t, q_t, k_t, v_t, lse, att_t = take(6)
    qkv_sources, out_sources = take(5), take(5)
    gain, cosine_ref, sine_ref, seg_col, seg_row = take(5)
    d_in, send, keep, gain_out = take(4)
    w_qkv, w_out, d_rows, d_norm_f, qkv_sems, out_sems = take(6)
    qkv_copies = start_qkv(place, qkv_sources, w_qkv, qkv_sems, q_cols, kv_cols)
    out_copies = start_out(place, out_sources, w_out, out_sems, o_cols)

    half = a.shape[0]
    d_norm_f[:half] = a[...].astype(F32) + a_in[...].astype(F32)
    d_norm_f[half:] = b[...].astype(F32) + b_in[...].astype(F32)
    middle = middle_ref[...]
    inv_f = inverse_rms(middle)
    d_normed_f = d_norm_f[...]
    gain_out[1:2] = jnp.sum(d_normed_f * middle * inv_f, axis=0, keepdims=True)
    scaled = d_normed_f * gain[1:2]
    d_middle = (
        upstream_ref[...].astype(F32)
        + inv_f * scaled
        - middle * (inv_f * inv_f * inv_f) * jnp.mean(scaled * middle, axis=-1, keepdims=True)
    )
    d_middle_b = d_middle.astype(BF)
    cosine, sine_table = cosine_ref[...], -sine_ref[...]
    allowed = allowed_rows(seg_col[...], seg_row[...])
    out_copies.wait()
    d_att = dot(d_middle_b, w_out[...], 1, 0).astype(BF).T
    q_rows, kv_rows = HQ * HD, KV * HD
    for kv in range(KV):
        key = kv * HD
        keys, values = k_t[key : key + HD], v_t[key : key + HD]
        d_keys = d_values = None
        for head in range(kv * GROUP, (kv + 1) * GROUP):
            at = head * HD
            queries = q_t[at : at + HD]
            scores = dot(keys, queries, 0, 0) * scale
            scores = jnp.where(allowed, scores, masked_score)
            probs = jnp.exp(scores - lse[head : head + 1])
            d_out = d_att[at : at + HD]
            delta = jnp.sum(
                d_out.astype(F32) * att_t[at : at + HD].astype(F32), axis=0, keepdims=True
            )
            d_probs = dot(values, d_out, 0, 0)
            d_scores = (probs * (d_probs - delta) * scale).astype(BF)
            d_queries = dot(keys, d_scores, 1, 0)
            d_rows[at : at + HD] = turn_rows(d_queries, cosine, sine_table, 1).astype(BF)
            key_part = dot(queries, d_scores, 1, 1)
            value_part = dot(d_out, probs.astype(BF), 1, 1)
            d_keys = key_part if d_keys is None else d_keys + key_part
            d_values = value_part if d_values is None else d_values + value_part
        at = q_rows + key
        d_rows[at : at + HD] = turn_rows(d_keys, cosine, sine_table, 1).astype(BF)
        d_rows[at + kv_rows : at + kv_rows + HD] = d_values.astype(BF)
    qkv_copies.wait()
    d_normed = dot(d_rows[...].T, w_qkv[...], 1, 0)
    x = x_ref[...].astype(F32)
    inv = inverse_rms(x)
    gain_out[0:1] = jnp.sum(d_normed * x * inv, axis=0, keepdims=True)
    scaled = d_normed * gain[0:1]
    d_in[...] = (
        d_middle
        + inv * scaled
        - x * (inv * inv * inv) * jnp.mean(scaled * x, axis=-1, keepdims=True)
    ).astype(BF)

    core, shard_at = place[0], place[1]
    rows_d = d_middle_b.shape[1]
    choose = (
        lax.broadcasted_iota(jnp.int32, (o_cols, rows_d), 1)
        == lax.broadcasted_iota(jnp.int32, (o_cols, rows_d), 0) + shard_at * o_cols
    )
    own_out = dot(jnp.where(choose, 1.0, 0.0).astype(BF), d_middle_b, 1, 1).astype(BF)
    own_q = d_rows[pl.ds(pl.multiple_of(shard_at * q_cols, 16), q_cols)]
    own_k = d_rows[pl.ds(pl.multiple_of(q_rows + shard_at * kv_cols, 16), kv_cols)]
    own_v = d_rows[pl.ds(pl.multiple_of(q_rows + kv_rows + shard_at * kv_cols, 16), kv_cols)]
    wide = normed_t.shape[0]
    send[:wide] = normed_t[...]
    last = 2 * wide

    @pl.when(core == 0)
    def _():
        keep[:q_cols] = own_q
        keep[q_cols:] = own_k
        send[wide:last] = att_t[...]
        send[last : last + o_cols] = own_out
        send[last + o_cols :] = own_v

    @pl.when(core != 0)
    def _():
        keep[:o_cols] = own_out
        keep[o_cols:] = own_v
        send[wide:last] = normed_t[...]
        send[last : last + q_cols] = own_q
        send[last + q_cols :] = own_k


def attention_grad_body(place, keep, normed_t, att_t, got, out):
    chunks, rows, wide = out.shape
    d_model = normed_t.shape[0]
    kv_cols = keep.shape[0] - wide * 3 // 4
    cols = wide - kv_cols
    second = dot(normed_t[...], keep[cols:], 1, 1) + dot(
        got[:d_model], got[2 * d_model + cols :], 1, 1
    )
    second = second.astype(BF)
    theirs = dot(got[d_model : 2 * d_model], got[2 * d_model : 2 * d_model + cols], 1, 1)

    def finish(mine):
        first = (dot(mine[...], keep[:cols], 1, 1) + theirs).astype(BF)
        for chunk in range(chunks):
            out[chunk, :, :cols] = first[chunk * rows : (chunk + 1) * rows]
            out[chunk, :, cols:] = second[chunk * rows : (chunk + 1) * rows]

    @pl.when(place[0] == 0)
    def _():
        finish(normed_t)

    @pl.when(place[0] != 0)
    def _():
        finish(att_t)


def turn_body(place, wq, wk, wv, wo, qkv, out):
    def eye(size):
        return jnp.where(
            lax.broadcasted_iota(jnp.int32, (size, size), 0)
            == lax.broadcasted_iota(jnp.int32, (size, size), 1),
            1.0,
            0.0,
        ).astype(BF)

    q_cols, kv_cols = wq.shape[1], wk.shape[1]
    qkv[:q_cols] = dot(eye(q_cols), wq[...], 1, 1).astype(BF)
    qkv[q_cols : q_cols + kv_cols] = dot(eye(kv_cols), wk[...], 1, 1).astype(BF)
    qkv[q_cols + kv_cols :] = dot(eye(kv_cols), wv[...], 1, 1).astype(BF)
    out[...] = dot(eye(wo.shape[1]), wo[...], 1, 1).astype(BF)


def swap(block, axis, bit):
    return lax.ppermute(block, axis, [(i, i ^ bit) for i in range(lax.axis_size(axis))])


def swap_chips(block):
    return lax.ppermute(
        block,
        ("section", "shard"),
        [(core * 4 + at, core * 4 + (at ^ (1 + core))) for core in range(2) for at in range(4)],
    )


def line_sum(block, axis):
    bit = 1
    while bit < lax.axis_size(axis):
        block = block + swap(block, axis, bit)
        bit *= 2
    return block


def rope_tables(segments):
    length = segments.shape[-1]
    position = jnp.arange(length, dtype=jnp.int32)
    before = jnp.concatenate([segments[:1] - 1, segments[:-1]])
    starts = jnp.where(segments != before, position, 0)
    starts = jnp.max(
        jnp.where(position[None, :] <= position[:, None], starts[None, :], 0), axis=1
    )
    places = (position - starts).astype(F32)
    frequency = rope_base ** (jnp.arange(HD // 2, dtype=F32) * (-2.0 / HD))
    angles = frequency[:, None] * places[None, :]
    return (jnp.cos(angles), jnp.sin(angles))


def local(
    inputs,
    cotangent,
    segments,
    attn_q,
    attn_k,
    attn_v,
    attn_out,
    ffn_gate,
    ffn_up,
    ffn_down,
    norm_gains,
):
    core = lax.axis_index("section")
    shard_at = lax.axis_index("shard")
    place = jnp.stack([core, shard_at]).astype(jnp.int32)
    first = core == 0
    block_len, d_model = inputs.shape[1:]
    replicas = lax.axis_size("replica")
    q_cols, kv_cols, o_cols = attn_q.shape[2], attn_k.shape[2], attn_out.shape[2]
    ff_cols = ffn_gate.shape[2]
    widths = (q_cols, kv_cols, o_cols)
    q_rows, kv_rows = 4 * q_cols, 4 * kv_cols

    def partner(block):
        return swap(block, "section", 1)

    def pick(zero, one):
        return jnp.where(first, zero, one)

    def mine(stacked):
        return lax.dynamic_index_in_dim(stacked, core, 0, keepdims=False)

    x0 = lax.all_gather(mine(inputs), "shard", axis=0, tiled=True)
    upstream = lax.all_gather(mine(cotangent), "shard", axis=0, tiled=True)
    length = x0.shape[0]

    qkv_own, out_own = call(
        turn_body,
        "turn",
        (place, attn_q[0], attn_k[0], attn_v[0], attn_out[0]),
        (shape((q_cols + 2 * kv_cols, d_model), BF), shape((o_cols, d_model), BF)),
    )

    def gathered(own):
        low = (own.shape[0] // 2 + 15) // 16 * 16
        one = swap_chips(own)
        two = partner(one)
        half = swap_chips(pick(two[:low], two[-low:]))
        return [own, one, two, half, partner(half)]

    qkv_other, out_other = partner(qkv_own), partner(out_own)
    qkv_layers = [gathered(pick(qkv_own, qkv_other)), None]
    out_layers = [gathered(pick(out_own, out_other)), None]
    qkv_layers[1] = gathered(pick(qkv_other, qkv_own))
    out_layers[1] = gathered(pick(out_other, out_own))
    ffn_sources = []
    for own in (ffn_gate[0], ffn_up[0], ffn_down[0]):
        ffn_sources += [own, partner(own)]
    gain_other = partner(norm_gains[0])
    gain_layers = [pick(norm_gains[0], gain_other), pick(gain_other, norm_gains[0])]

    seg = mine(segments)
    tables = rope_tables(seg) + (seg[:, None], seg[None, :])

    attn_scratch = (
        pltpu.VMEM((q_rows + 2 * kv_rows, d_model), BF),
        pltpu.VMEM((4 * o_cols, d_model), BF),
    )
    ffn_scratch = (
        pltpu.VMEM((d_model, ff_cols), BF),
        pltpu.VMEM((d_model, ff_cols), BF),
        pltpu.VMEM((ff_cols, d_model), BF),
    )
    qkv_sems = pltpu.SemaphoreType.DMA((20,))
    out_sems = pltpu.SemaphoreType.DMA((8,))
    ffn_sems = pltpu.SemaphoreType.DMA((6,))
    half_rows = shape((length // 2, d_model), BF)

    def forward(layer, entry):
        arrays = (place, *entry, *qkv_layers[layer], *out_layers[layer], *ffn_sources)
        start = 1 + len(entry)
        outs = [
            shape((d_model, length), BF),
            shape((q_rows, length), BF),
            shape((kv_rows, length), BF),
            shape((kv_rows, length), BF),
            shape((16, length), F32),
            shape((q_rows, length), BF),
            shape((length, d_model), F32),
            shape((length, d_model), BF),
            shape((length, ff_cols), F32),
            shape((length, ff_cols), F32),
            shape((length, ff_cols), BF),
        ]
        if layer:
            outs = [shape((length, d_model), BF)] + outs + [shape((length, d_model), BF)]
        else:
            outs = outs + [half_rows, half_rows]
        return call(
            functools.partial(forward_body, layer, widths),
            "forward",
            arrays + (gain_layers[layer],) + tables,
            outs,
            attn_scratch + ffn_scratch + (qkv_sems, out_sems, ffn_sems),
            range(start, start + 16),
        )

    def exchange(a, b):
        a_in, b_in = swap(a, "shard", 1), swap(b, "shard", 2)
        a = (a.astype(F32) + a_in.astype(F32)).astype(BF)
        b = (b.astype(F32) + b_in.astype(F32)).astype(BF)
        return a, swap(a, "shard", 2), b, swap(b, "shard", 1)

    def own_rows(full):
        return lax.dynamic_slice_in_dim(full, shard_at * block_len, block_len, 0)

    *saved0, part_a, part_b = forward(0, (x0,))
    x1, *saved1, part = forward(1, (saved0[6], *exchange(part_a, part_b)))
    xs, saved = (x0, x1), (saved0, saved1)

    side, low = shard_at // 2, shard_at % 2
    two_blocks = 2 * block_len
    near = lax.dynamic_slice_in_dim(part, side * two_blocks, two_blocks, 0)
    far = lax.dynamic_slice_in_dim(part, (1 - side) * two_blocks, two_blocks, 0)
    near = near.astype(F32) + swap(far, "shard", 2).astype(F32)
    mine_block = lax.dynamic_slice_in_dim(near, low * block_len, block_len, 0)
    sent = lax.dynamic_slice_in_dim(near, (1 - low) * block_len, block_len, 0).astype(BF)
    total = mine_block + swap(sent, "shard", 1).astype(F32)
    own_out = [own_rows(x1), (own_rows(saved1[6]) + total).astype(BF)]

    own_grads, gains_out = [None, None], [None, None]
    ffn_reduced, attn_reduced = [None, None], [None, None]
    chunk_rows = d_model // replicas

    def reduce(chunks):
        return lax.psum_scatter(chunks, "replica", scatter_dimension=0, tiled=False)

    for layer in (1, 0):
        (normed_t, q_t, k_t, v_t, lse, att_t, middle, normed_f, gate_pre, up_pre, hidden) = saved[layer]
        send, keep, part_a, part_b = call(
            functools.partial(ffn_backward_body, layer),
            "ffn_backward",
            (place, upstream, gate_pre, up_pre, hidden, normed_f, *ffn_sources),
            (
                shape((3, length, d_model), BF),
                shape((length, 3 * (ff_cols // 2)), BF),
                half_rows,
                half_rows,
            ),
            ffn_scratch + (ffn_sems,),
            range(6, 12),
        )
        sums = exchange(part_a, part_b)
        (ffn_chunks,) = call(
            ffn_grad_body,
            "ffn_grad",
            (place, keep, normed_f, upstream, partner(send)),
            (shape((replicas, chunk_rows, 3 * (ff_cols // 2)), BF),),
        )
        ffn_reduced[layer] = reduce(ffn_chunks)
        wide = o_cols + kv_cols
        upstream, send, keep, gains_out[layer] = call(
            functools.partial(attention_backward_body, widths),
            "attention_backward",
            (place, *sums, upstream, middle, xs[layer], normed_t, q_t, k_t, v_t, lse, att_t)
            + (*qkv_layers[layer], *out_layers[layer], gain_layers[layer])
            + tables,
            (
                shape((length, d_model), BF),
                shape((2 * d_model + wide, length), BF),
                shape((wide, length), BF),
                shape((2, d_model), F32),
            ),
            attn_scratch
            + (
                pltpu.VMEM((q_rows + 2 * kv_rows, length), BF),
                pltpu.VMEM((length, d_model), F32),
                qkv_sems,
                out_sems,
            ),
            range(14, 24),
        )
        (attn_chunks,) = call(
            attention_grad_body,
            "attention_grad",
            (place, keep, normed_t, att_t, partner(send)),
            (shape((replicas, chunk_rows, wide), BF),),
        )
        attn_reduced[layer] = reduce(attn_chunks)
        own_grads[layer] = own_rows(upstream)

    def to_owner(zero, one):
        got = partner(pick(one, zero))
        return pick(zero, got), pick(got, one)

    acts = jnp.stack(to_owner(own_out[0], own_out[1]))
    grads = jnp.stack(to_owner(own_grads[0], own_grads[1]))
    ffn_lo, ffn_hi = to_owner(ffn_reduced[0], ffn_reduced[1])
    attn_lo, attn_hi = to_owner(attn_reduced[0], attn_reduced[1])
    half = ff_cols // 2

    def halves(start):
        return jnp.concatenate(
            [ffn_lo[:, start : start + half], ffn_hi[:, start : start + half]], axis=1
        ).astype(F32)

    final_gate, final_up = halves(0), halves(half)
    final_down = halves(2 * half).T
    final_q, final_k = attn_lo[:, :q_cols].astype(F32), attn_lo[:, q_cols:].astype(F32)
    final_out, final_v = attn_hi[:, :o_cols].astype(F32), attn_hi[:, o_cols:].astype(F32)
    gain_parts = to_owner(gains_out[0], gains_out[1])
    gains_total = line_sum(gain_parts[0] + gain_parts[1], "replica")
    return (
        acts[None],
        grads[None],
        final_q[None],
        final_k[None],
        final_v[None],
        final_out[None],
        final_gate[None],
        final_up[None],
        final_down[None],
        gains_total[None],
    )


def solution(mesh):
    placed = (
        P("replica", "shard", None),
        P("replica", "shard", None),
        P("replica", None),
        P("section", None, "shard"),
        P("section", None, "shard"),
        P("section", None, "shard"),
        P("section", None, "shard"),
        P("section", None, "shard"),
        P("section", None, "shard"),
        P("section", "shard", None),
        P("section", None, None),
    )
    return jax.shard_map(
        local,
        mesh=mesh,
        in_specs=placed,
        out_specs=(
            P("section", "replica", "shard", None),
            P("section", "replica", "shard", None),
            P("section", "replica", "shard"),
            P("section", "replica", "shard"),
            P("section", "replica", "shard"),
            P("section", "replica", "shard"),
            P("section", "replica", "shard"),
            P("section", "replica", "shard"),
            P("section", "shard", "replica"),
            P("section", None, None),
        ),
        check_vma=False,
    )
```

```python
import functools

import jax
import jax.numpy as jnp
from jax import lax
from jax.experimental import pallas as pl
from jax.experimental.pallas import tpu as pltpu
from jax.sharding import PartitionSpec as P

HQ = 15
KV = 5
HD = 64
GROUP = HQ // KV

epsilon = 1e-05
rope_base = 10000.0
masked_score = -1e30
scale = HD**-0.5
spare = 16

BF = jnp.bfloat16
F32 = jnp.float32


def dot(left, right, left_dim, right_dim):
    return lax.dot_general(
        left, right, (((left_dim,), (right_dim,)), ((), ())), preferred_element_type=F32
    )


def shape(dims, dtype):
    return jax.ShapeDtypeStruct(dims, dtype)


def call(body, name, arrays, outs, scratch=(), in_hbm=()):
    specs = [pl.BlockSpec(memory_space=pltpu.SMEM)] + [
        pl.BlockSpec(memory_space=pl.ANY if at in in_hbm else pltpu.VMEM)
        for at in range(1, len(arrays))
    ]
    return pl.pallas_call(
        body,
        name=name,
        in_specs=specs,
        out_specs=[pl.BlockSpec(memory_space=pltpu.VMEM) for _ in outs],
        out_shape=list(outs),
        scratch_shapes=list(scratch),
        compiler_params=pltpu.CompilerParams(vmem_limit_bytes=60 * 1024 * 1024),
    )(*arrays)


class Copies:
    def __init__(self, sems):
        self.sems, self.plain, self.cond = sems, [], []
        self.used = 0

    def _make(self, source, target):
        sem = self.sems.at[self.used]
        self.used += 1
        return pltpu.make_async_copy(source, target, sem)

    def add(self, source, target):
        copy = self._make(source, target)
        copy.start()
        self.plain.append(copy)

    def add_when(self, cond, pairs):
        made = [self._make(source, target) for source, target in pairs]

        @pl.when(cond)
        def _():
            for copy in made:
                copy.start()

        self.cond.append((cond, made))

    def wait(self):
        for copy in self.plain:
            copy.wait()
        for cond, made in self.cond:

            @pl.when(cond)
            def _(made=made):
                for copy in made:
                    copy.wait()


def start_pieces(place, sources, pieces, sems):
    core, shard_at = place[0], place[1]
    own, one, two, half, half_other = sources
    low, total = half.shape[0], own.shape[0]
    copies = Copies(sems)

    def rows(block, source, first, last, source_first):
        out = []
        for start, size, target, base in pieces:
            lo, hi = max(start, first), min(start + size, last)
            if lo < hi:
                at = pl.multiple_of(base + block * size + (lo - start), 16)
                out.append(
                    (
                        source.at[pl.ds(lo - source_first, hi - lo)],
                        target.at[pl.ds(at, hi - lo)],
                    )
                )
        return out

    for block, source in (
        (shard_at, own),
        (shard_at ^ (1 + core), one),
        (shard_at ^ (2 - core), two),
    ):
        for pair in rows(block, source, 0, total, 0):
            copies.add(*pair)
    across = shard_at ^ 3
    for at in range(2):
        top, bottom = (half, half_other) if at == 0 else (half_other, half)
        copies.add_when(
            core == at,
            rows(across, top, 0, low, 0) + rows(across, bottom, low, total, total - low),
        )
    return copies


def start_qkv(place, sources, target, sems, widths):
    q_cols, kv_cols, _ = widths
    pieces = (
        (0, q_cols, target, 0),
        (q_cols, kv_cols, target, 4 * q_cols),
        (q_cols + kv_cols, kv_cols, target, 4 * (q_cols + kv_cols)),
    )
    return start_pieces(place, sources, pieces, sems)


def start_out(place, sources, target, sems, widths):
    q_cols, kv_cols, o_cols = widths
    first = q_cols + 2 * kv_cols
    return start_pieces(place, sources, ((first, o_cols, target, 0),), sems)


def start_ffn(place, layer, sources, targets, sems):
    copies = Copies(sems)
    for (own, other), target in zip(sources, targets):
        copies.add_when(place[0] == layer, [(own, target)])
        copies.add_when(place[0] != layer, [(other, target)])
    return copies


def turn_rows(values, cosine, sine_table, heads):
    half = HD // 2
    out = []
    for head in range(heads):
        a = values[head * HD : head * HD + half]
        b = values[head * HD + half : (head + 1) * HD]
        out.append(a * cosine - b * sine_table)
        out.append(b * cosine + a * sine_table)
    return jnp.concatenate(out, axis=0)


def allowed_rows(seg_col, seg_row):
    length = seg_col.shape[0]
    key_at = lax.broadcasted_iota(jnp.int32, (length, length), 0)
    query_at = lax.broadcasted_iota(jnp.int32, (length, length), 1)
    return (seg_col == seg_row) & (key_at <= query_at)


def inverse_rms(values):
    return lax.rsqrt(jnp.mean(values * values, axis=-1, keepdims=True) + epsilon)


def place_rows(place, sources, target):
    for at, source in enumerate(sources):
        rows = source.shape[0]
        target[pl.ds(pl.multiple_of((place[1] ^ at) * rows, 16), rows)] = source[...]


def forward_body(layer, widths, place, *refs):
    refs = list(refs)

    def take(count):
        out = refs[:count]
        del refs[:count]
        return out

    if layer:
        before, a, a_in, b, b_in = take(5)
    else:
        x_sources = take(4)
    attn_sources = take(5)
    ffn_sources = [take(2) for _ in range(3)]
    gain, cosine_ref, sine_ref, seg_col, seg_row = take(5)
    x_out, normed_t, q_t, k_t, v_t, lse, att_t = take(7)
    middle_out, normed_f_out, gate_out, up_out, hidden_out = take(5)
    parts = take(1 if layer else 2)
    w_qkv, w_out, w_gate, w_up, w_down, qkv_sems, out_sems, ffn_sems = take(8)
    qkv_copies = start_qkv(place, attn_sources, w_qkv, qkv_sems, widths)
    out_copies = start_out(place, attn_sources, w_out, out_sems, widths)
    ffn_copies = start_ffn(place, layer, ffn_sources, (w_gate, w_up, w_down), ffn_sems)
    if layer:
        half = a.shape[0]
        x_out[:half] = (before[:half] + (a[...].astype(F32) + a_in[...].astype(F32))).astype(BF)
        x_out[half:] = (before[half:] + (b[...].astype(F32) + b_in[...].astype(F32))).astype(BF)
    else:
        place_rows(place, x_sources, x_out)
    x = x_out[...].astype(F32)
    normed = (x * inverse_rms(x) * gain[0:1]).astype(BF)
    normed_t[...] = normed.T
    cosine, sine_table = cosine_ref[...], sine_ref[...]
    allowed = allowed_rows(seg_col[...], seg_row[...])
    qkv_copies.wait()
    q_rows, kv_rows = HQ * HD, KV * HD
    qkv = dot(w_qkv[...], normed, 1, 1)
    q_t[...] = turn_rows(qkv[:q_rows], cosine, sine_table, HQ).astype(BF)
    k_t[...] = turn_rows(qkv[q_rows : q_rows + kv_rows], cosine, sine_table, KV).astype(BF)
    v_t[...] = qkv[q_rows + kv_rows :].astype(BF)
    lse[...] = jnp.zeros(lse.shape, F32)
    for head in range(HQ):
        key = (head // GROUP) * HD
        scores = dot(k_t[key : key + HD], q_t[head * HD : (head + 1) * HD], 0, 0) * scale
        scores = jnp.where(allowed, scores, masked_score)
        top = jnp.max(scores, axis=0, keepdims=True)
        weight = jnp.exp(scores - top)
        total = jnp.sum(weight, axis=0, keepdims=True)
        lse[head : head + 1] = top + jnp.log(total)
        probs = (weight * (1.0 / total)).astype(BF)
        att_t[head * HD : (head + 1) * HD] = dot(v_t[key : key + HD], probs, 1, 0).astype(BF)
    attended = att_t[...].T
    out_copies.wait()
    middle = x + dot(attended, w_out[...], 1, 1)
    middle_out[...] = middle
    normed_f = (middle * inverse_rms(middle) * gain[1:2]).astype(BF)
    normed_f_out[...] = normed_f
    ffn_copies.wait()
    gate_pre = dot(normed_f, w_gate[...], 1, 0)
    up_pre = dot(normed_f, w_up[...], 1, 0)
    gate_out[...] = gate_pre
    up_out[...] = up_pre
    hidden = (gate_pre / (1.0 + jnp.exp(-gate_pre)) * up_pre).astype(BF)
    hidden_out[...] = hidden
    part = dot(hidden, w_down[...], 1, 1).astype(BF)
    if layer:
        parts[0][...] = part
    else:
        half = part.shape[0] // 2
        parts[0][...] = part[:half]
        parts[1][...] = part[half:]


def ffn_backward_body(layer, place, *refs):
    refs = list(refs)

    def take(count):
        out = refs[:count]
        del refs[:count]
        return out

    up_sources = take(4 if layer else 1)
    gate_ref, up_ref, hidden_ref, normed_ref = take(4)
    sources = [take(2) for _ in range(3)]
    send, keep, part_a, part_b = take(4)
    if layer:
        (upstream_ref,) = take(1)
        place_rows(place, up_sources, upstream_ref)
    else:
        (upstream_ref,) = up_sources
    w_gate, w_up, w_down, sems = take(4)
    copies = start_ffn(place, layer, sources, (w_gate, w_up, w_down), sems)
    upstream, gate_pre, up_pre = upstream_ref[...], gate_ref[...], up_ref[...]
    length = upstream.shape[0]
    send[length : 2 * length] = normed_ref[...]
    send[2 * length : 3 * length] = upstream
    send[3 * length :] = jnp.zeros((spare, upstream.shape[1]), BF)
    copies.wait()
    d_hidden = dot(upstream, w_down[...], 1, 0)
    sigma = 1.0 / (1.0 + jnp.exp(-gate_pre))
    d_gate = (d_hidden * up_pre * sigma * (1.0 + gate_pre * (1.0 - sigma))).astype(BF)
    d_up = (d_hidden * gate_pre * sigma).astype(BF)
    part = (dot(d_gate, w_gate[...], 1, 1) + dot(d_up, w_up[...], 1, 1)).astype(BF)
    half = part.shape[0] // 2
    part_a[...] = part[:half]
    part_b[...] = part[half:]
    wide = d_gate.shape[1] // 2
    blocks = (d_gate, d_up, hidden_ref[...])
    low = jnp.concatenate([block[:, :wide] for block in blocks], axis=1)
    high = jnp.concatenate([block[:, wide:] for block in blocks], axis=1)
    is_low = place[0] == 0

    @pl.when(is_low)
    def _():
        keep[...] = low
        send[:length] = high

    @pl.when(jnp.logical_not(is_low))
    def _():
        keep[...] = high
        send[:length] = low


def ffn_grad_body(place, keep, normed, upstream, got, *rest):
    *rider, out = rest
    chunks, rows, _ = out.shape
    wide = keep.shape[1]
    two_thirds = wide * 2 // 3
    length = keep.shape[0]
    got_normed, got_up = got[length : 2 * length], got[2 * length : 3 * length]
    first = dot(normed[...], keep[:, :two_thirds], 0, 0) + dot(
        got_normed, got[:length, :two_thirds], 0, 0
    )
    second = dot(upstream[...], keep[:, two_thirds:], 0, 0) + dot(
        got_up, got[:length, two_thirds:], 0, 0
    )
    both = jnp.concatenate([first, second], axis=1).astype(BF)
    if rider:
        out[:, :, wide:] = rider[0][...]
    for chunk in range(chunks):
        out[chunk, :, :wide] = both[chunk * rows : (chunk + 1) * rows]


def attention_backward_body(widths, place, *refs):
    refs = list(refs)

    def take(count):
        out = refs[:count]
        del refs[:count]
        return out

    q_cols, kv_cols, o_cols = widths
    a, a_in, b, b_in, upstream_ref, middle_ref, x_ref = take(7)
    normed_t, q_t, k_t, v_t, lse, att_t = take(6)
    attn_sources = take(5)
    gain, cosine_ref, sine_ref, seg_col, seg_row = take(5)
    d_in, send, keep, gain_out = take(4)
    w_qkv, w_out, d_rows, d_norm_f, qkv_sems, out_sems = take(6)
    out_copies = start_out(place, attn_sources, w_out, out_sems, widths)
    qkv_copies = start_qkv(place, attn_sources, w_qkv, qkv_sems, widths)

    half = a.shape[0]
    d_norm_f[:half] = a[...].astype(F32) + a_in[...].astype(F32)
    d_norm_f[half:] = b[...].astype(F32) + b_in[...].astype(F32)
    middle = middle_ref[...]
    inv_f = inverse_rms(middle)
    d_normed_f = d_norm_f[...]
    gain_out[1:2] = jnp.sum(d_normed_f * middle * inv_f, axis=0, keepdims=True)
    scaled = d_normed_f * gain[1:2]
    d_middle = (
        upstream_ref[...].astype(F32)
        + inv_f * scaled
        - middle * (inv_f * inv_f * inv_f) * jnp.mean(scaled * middle, axis=-1, keepdims=True)
    )
    d_middle_b = d_middle.astype(BF)
    cosine, sine_table = cosine_ref[...], -sine_ref[...]
    allowed = allowed_rows(seg_col[...], seg_row[...])
    out_copies.wait()
    d_att = dot(d_middle_b, w_out[...], 1, 0).astype(BF).T
    q_rows, kv_rows = HQ * HD, KV * HD
    for kv in range(KV):
        key = kv * HD
        keys, values = k_t[key : key + HD], v_t[key : key + HD]
        d_keys = d_values = None
        for head in range(kv * GROUP, (kv + 1) * GROUP):
            at = head * HD
            queries = q_t[at : at + HD]
            scores = dot(keys, queries, 0, 0) * scale
            scores = jnp.where(allowed, scores, masked_score)
            probs = jnp.exp(scores - lse[head : head + 1])
            d_out = d_att[at : at + HD]
            delta = jnp.sum(
                d_out.astype(F32) * att_t[at : at + HD].astype(F32), axis=0, keepdims=True
            )
            d_probs = dot(values, d_out, 0, 0)
            d_scores = (probs * (d_probs - delta) * scale).astype(BF)
            d_queries = dot(keys, d_scores, 1, 0)
            d_rows[at : at + HD] = turn_rows(d_queries, cosine, sine_table, 1).astype(BF)
            key_part = dot(queries, d_scores, 1, 1)
            value_part = dot(d_out, probs.astype(BF), 1, 1)
            d_keys = key_part if d_keys is None else d_keys + key_part
            d_values = value_part if d_values is None else d_values + value_part
        at = q_rows + key
        d_rows[at : at + HD] = turn_rows(d_keys, cosine, sine_table, 1).astype(BF)
        d_rows[at + kv_rows : at + kv_rows + HD] = d_values.astype(BF)
    qkv_copies.wait()
    d_normed = dot(d_rows[...].T, w_qkv[...], 1, 0)
    x = x_ref[...].astype(F32)
    inv = inverse_rms(x)
    gain_out[0:1] = jnp.sum(d_normed * x * inv, axis=0, keepdims=True)
    scaled = d_normed * gain[0:1]
    d_in[...] = (
        d_middle
        + inv * scaled
        - x * (inv * inv * inv) * jnp.mean(scaled * x, axis=-1, keepdims=True)
    ).astype(BF)

    core, shard_at = place[0], place[1]
    rows_d = d_middle_b.shape[1]
    choose = (
        lax.broadcasted_iota(jnp.int32, (o_cols, rows_d), 1)
        == lax.broadcasted_iota(jnp.int32, (o_cols, rows_d), 0) + shard_at * o_cols
    )
    own_out = dot(jnp.where(choose, 1.0, 0.0).astype(BF), d_middle_b, 1, 1).astype(BF)
    own_q = d_rows[pl.ds(pl.multiple_of(shard_at * q_cols, 16), q_cols)]
    own_k = d_rows[pl.ds(pl.multiple_of(q_rows + shard_at * kv_cols, 16), kv_cols)]
    own_v = d_rows[pl.ds(pl.multiple_of(q_rows + kv_rows + shard_at * kv_cols, 16), kv_cols)]
    wide = normed_t.shape[0]
    send[:wide] = normed_t[...]
    last = 2 * wide

    @pl.when(core == 0)
    def _():
        keep[:q_cols] = own_q
        keep[q_cols:] = own_k
        send[wide:last] = att_t[...]
        send[last : last + o_cols] = own_out
        send[last + o_cols :] = own_v

    @pl.when(core != 0)
    def _():
        keep[:o_cols] = own_out
        keep[o_cols:] = own_v
        send[wide:last] = normed_t[...]
        send[last : last + q_cols] = own_q
        send[last + q_cols :] = own_k


def attention_grad_body(place, keep, normed_t, att_t, got, *rest):
    *gains, out = rest
    chunks, all_rows, width = out.shape
    rows = normed_t.shape[0] // chunks
    d_model = normed_t.shape[0]
    wide = keep.shape[0]
    cols = wide * 3 // 4
    second = dot(normed_t[...], keep[cols:], 1, 1) + dot(
        got[:d_model], got[2 * d_model + cols :], 1, 1
    )
    second = second.astype(BF)
    theirs = dot(got[d_model : 2 * d_model], got[2 * d_model : 2 * d_model + cols], 1, 1)

    if gains:
        out[:, :, wide:] = jnp.zeros((chunks, all_rows, width - wide), BF)
        values = jnp.concatenate([part[...] for part in gains], axis=0)
        high = values.astype(BF).astype(F32)
        both = jnp.concatenate([high, values - high], axis=0)
        both = jnp.concatenate([both, jnp.zeros((both.shape[0], 3 * width - d_model), F32)], axis=1)
        lines = [both[:, at * width : (at + 1) * width] for at in range(3)]
        lines.append(jnp.zeros((all_rows - rows - 3 * both.shape[0], width), F32))
        block = jnp.concatenate(lines, axis=0).astype(BF)
        for chunk in range(chunks):
            out[chunk, rows:] = block

    def finish(mine):
        first = (dot(mine[...], keep[:cols], 1, 1) + theirs).astype(BF)
        for chunk in range(chunks):
            out[chunk, :rows, :cols] = first[chunk * rows : (chunk + 1) * rows]
            out[chunk, :rows, cols:wide] = second[chunk * rows : (chunk + 1) * rows]

    @pl.when(place[0] == 0)
    def _():
        finish(normed_t)

    @pl.when(place[0] != 0)
    def _():
        finish(att_t)


def turn_body(layer, flips, place, *refs):
    out = refs[-1]

    def fill(which):
        at = 0
        for index, flip in enumerate(flips):
            weight = refs[2 * index + which]
            if flip:
                cols = weight.shape[1]
                same = lax.broadcasted_iota(jnp.int32, (cols, cols), 0) == (
                    lax.broadcasted_iota(jnp.int32, (cols, cols), 1)
                )
                block = dot(jnp.where(same, 1.0, 0.0).astype(BF), weight[...], 1, 1).astype(BF)
            else:
                block = weight[...]
            out[at : at + block.shape[0]] = block
            at += block.shape[0]
        out[at:] = jnp.zeros((out.shape[0] - at, out.shape[1]), BF)

    @pl.when(place[0] == layer)
    def _():
        fill(0)

    @pl.when(place[0] != layer)
    def _():
        fill(1)


def after(value, before):
    return pl.pallas_call(
        lambda value, before, out: None,
        name="after",
        in_specs=[pl.BlockSpec(memory_space=pl.ANY)] * 2,
        out_specs=pl.BlockSpec(memory_space=pl.ANY),
        out_shape=shape(value.shape, value.dtype),
        input_output_aliases={0: 0},
    )(value, before)


def tie(value, *before):
    return lax.optimization_barrier((value, *before))[0]


def swap(block, axis, bit):
    return lax.ppermute(block, axis, [(i, i ^ bit) for i in range(lax.axis_size(axis))])


def swap_chips(block):
    return lax.ppermute(
        block,
        ("section", "shard"),
        [(core * 4 + at, core * 4 + (at ^ (1 + core))) for core in range(2) for at in range(4)],
    )


def rope_tables(segments):
    length = segments.shape[-1]
    position = jnp.arange(length, dtype=jnp.int32)
    before = jnp.concatenate([segments[:1] - 1, segments[:-1]])
    starts = jnp.where(segments != before, position, 0)
    starts = jnp.max(
        jnp.where(position[None, :] <= position[:, None], starts[None, :], 0), axis=1
    )
    places = (position - starts).astype(F32)
    frequency = rope_base ** (jnp.arange(HD // 2, dtype=F32) * (-2.0 / HD))
    angles = frequency[:, None] * places[None, :]
    return (jnp.cos(angles), jnp.sin(angles))


def local(
    inputs,
    cotangent,
    segments,
    attn_q,
    attn_k,
    attn_v,
    attn_out,
    ffn_gate,
    ffn_up,
    ffn_down,
    norm_gains,
):
    core = lax.axis_index("section")
    shard_at = lax.axis_index("shard")
    place = jnp.stack([core, shard_at]).astype(jnp.int32)
    first = core == 0
    block_len, d_model = inputs.shape[1:]
    replicas = lax.axis_size("replica")
    q_cols, kv_cols, o_cols = attn_q.shape[2], attn_k.shape[2], attn_out.shape[2]
    ff_cols = ffn_gate.shape[2]
    widths = (q_cols, kv_cols, o_cols)
    q_rows, kv_rows = 4 * q_cols, 4 * kv_cols

    def partner(block):
        return swap(block, "section", 1)

    def pick(zero, one):
        return jnp.where(first, zero, one)

    def mine(stacked):
        return lax.dynamic_index_in_dim(stacked, core, 0, keepdims=False)

    length = 4 * block_len

    def gathered_rows(own):
        return [own] + [swap(own, "shard", bit) for bit in (1, 2, 3)]

    def turned(layer, weights, flips):
        rows = sum(own.shape[1 if flip else 0] for (own, _), flip in zip(weights, flips))
        (out,) = call(
            functools.partial(turn_body, layer, flips),
            "turn",
            (place, *[array for pair in weights for array in pair]),
            (shape((rows + spare, d_model), BF),),
        )
        return out

    def start_gather(own, one, before=(), last=()):
        two = partner(one)
        low = (own.shape[0] // 2 + 15) // 16 * 16
        sent = lax.dynamic_slice_in_dim(two, core * (own.shape[0] - low), low, 0)
        half = swap_chips(tie(sent, *before) if before else sent)
        return [own, one, two, half, partner(tie(half, *last) if last else half)]

    seg = mine(segments)
    tables = rope_tables(seg) + (seg[:, None], seg[None, :])

    gain_other = partner(norm_gains[0])
    gain_layers = [pick(norm_gains[0], gain_other), pick(gain_other, norm_gains[0])]
    x_sources = gathered_rows(mine(inputs))
    pairs = [(own, partner(own)) for own in (attn_q[0], attn_k[0].T, attn_v[0].T, attn_out[0])]
    flips = (True, False, False, True)
    rows0 = turned(0, pairs, flips)
    rows1 = turned(1, [(tie(own, rows0), other) for own, other in pairs], flips)
    one0, *settled = lax.optimization_barrier(
        (swap_chips(tie(rows0, *x_sources[1:])), rows1, *tables, *gain_layers)
    )
    tables, gain_layers = tuple(settled[1:5]), settled[5:]
    attn0 = start_gather(rows0, one0)
    ffn_sources = []
    for own in (ffn_gate[0], ffn_up[0], ffn_down[0].T):
        ffn_sources += [own, partner(tie(own, rows0))]
    one1 = swap_chips(tie(rows1, attn0[3]))

    attn_scratch = (
        pltpu.VMEM((q_rows + 2 * kv_rows, d_model), BF),
        pltpu.VMEM((4 * o_cols, d_model), BF),
    )
    ffn_scratch = (
        pltpu.VMEM((d_model, ff_cols), BF),
        pltpu.VMEM((d_model, ff_cols), BF),
        pltpu.VMEM((d_model, ff_cols), BF),
    )
    qkv_sems = pltpu.SemaphoreType.DMA((20,))
    out_sems = pltpu.SemaphoreType.DMA((8,))
    ffn_sems = pltpu.SemaphoreType.DMA((6,))
    half_rows = shape((length // 2, d_model), BF)

    def forward(layer, entry):
        parts = [shape((length, d_model), BF)] if layer else [half_rows, half_rows]
        start = 1 + len(entry)
        return call(
            functools.partial(forward_body, layer, widths),
            "forward",
            (place, *entry, *attn_layers[layer], *ffn_sources, gain_layers[layer], *tables),
            [
                shape((length, d_model), BF),
                shape((d_model, length), BF),
                shape((q_rows, length), BF),
                shape((kv_rows, length), BF),
                shape((kv_rows, length), BF),
                shape((16, length), F32),
                shape((q_rows, length), BF),
                shape((length, d_model), F32),
                shape((length, d_model), BF),
                shape((length, ff_cols), F32),
                shape((length, ff_cols), F32),
                shape((length, ff_cols), BF),
            ]
            + parts,
            attn_scratch + ffn_scratch + (qkv_sems, out_sems, ffn_sems),
            range(start, start + 11),
        )

    def exchange(a, b):
        a_in, b_in = swap(a, "shard", 1), swap(b, "shard", 2)
        a = (a.astype(F32) + a_in.astype(F32)).astype(BF)
        b = (b.astype(F32) + b_in.astype(F32)).astype(BF)
        return (a, swap(a, "shard", 2), b, swap(b, "shard", 1)), a_in

    def own_rows(full):
        return lax.dynamic_slice_in_dim(full, shard_at * block_len, block_len, 0)

    attn_layers = [attn0, None]
    x0, *saved0, part_a, part_b = forward(0, x_sources)
    summed, received = exchange(part_a, part_b)
    attn_layers[1] = start_gather(rows1, tie(one1, part_a), (received,), (summed[1], summed[3]))
    cot_sources = gathered_rows(tie(mine(cotangent), attn_layers[1][3]))
    x1, *saved1, part = forward(1, (saved0[6], *summed))
    xs, saved = (x0, x1), (saved0, saved1)

    side, low = shard_at // 2, shard_at % 2
    two_blocks = 2 * block_len
    near = lax.dynamic_slice_in_dim(part, side * two_blocks, two_blocks, 0)
    far = lax.dynamic_slice_in_dim(part, (1 - side) * two_blocks, two_blocks, 0)
    near = near.astype(F32) + swap(far, "shard", 2).astype(F32)
    mine_block = lax.dynamic_slice_in_dim(near, low * block_len, block_len, 0)
    sent = lax.dynamic_slice_in_dim(near, (1 - low) * block_len, block_len, 0).astype(BF)
    total = mine_block + swap(sent, "shard", 1).astype(F32)
    own_out = [own_rows(x1), (own_rows(saved1[6]) + total).astype(BF)]

    def to_owner(zero, one):
        got = partner(pick(one, zero))
        return pick(zero, got), pick(got, one)

    own_grads, gains_out = [None, None], [None, None]
    reduced = []
    chunk_rows = d_model // replicas

    def reduce(chunks):
        return lax.psum_scatter(chunks, "replica", scatter_dimension=0, tiled=False)

    for layer in (1, 0):
        (normed_t, q_t, k_t, v_t, lse, att_t, middle, normed_f, gate_pre, up_pre, hidden) = saved[layer]
        entry = cot_sources if layer else [upstream]
        half_ff = 3 * (ff_cols // 2)
        send, keep, part_a, part_b, *assembled = call(
            functools.partial(ffn_backward_body, layer),
            "ffn_backward",
            (place, *entry, gate_pre, up_pre, hidden, normed_f, *ffn_sources),
            [
                shape((3 * length + spare, d_model), BF),
                shape((length, half_ff), BF),
                half_rows,
                half_rows,
            ]
            + ([shape((length, d_model), BF)] if layer else []),
            ffn_scratch + (ffn_sems,),
            range(5 + len(entry), 11 + len(entry)),
        )
        if layer:
            (upstream,) = assembled
        sums, _ = exchange(part_a, part_b)
        got = partner(send)
        rider = () if layer else (attn_chunks,)
        (ffn_chunks,) = call(
            ffn_grad_body,
            "ffn_grad",
            (place, keep, normed_f, upstream, got, *rider),
            (shape((replicas, chunk_rows, half_ff + (0 if layer else o_cols + kv_cols)), BF),),
        )
        if layer:
            reduced.append(reduce(ffn_chunks))
        else:
            ffn_chunks = after(ffn_chunks, reduced[0])
            reduced.append(reduce(ffn_chunks))
        sums = [tie(sums[0], ffn_chunks), *sums[1:]]
        wide = o_cols + kv_cols
        upstream, send, keep, gains_out[layer] = call(
            functools.partial(attention_backward_body, widths),
            "attention_backward",
            (place, *sums, upstream, middle, xs[layer], normed_t, q_t, k_t, v_t, lse, att_t)
            + (*attn_layers[layer], gain_layers[layer])
            + tables,
            (
                shape((length, d_model), BF),
                shape((2 * d_model + wide, length), BF),
                shape((wide, length), BF),
                shape((2, d_model), F32),
            ),
            attn_scratch
            + (
                pltpu.VMEM((q_rows + 2 * kv_rows, length), BF),
                pltpu.VMEM((length, d_model), F32),
                qkv_sems,
                out_sems,
            ),
            range(14, 19),
        )
        width = wide if layer else (wide + 127) // 128 * 128
        gains = () if layer else tuple(gains_out)
        (attn_chunks,) = call(
            attention_grad_body,
            "attention_grad",
            (place, keep, normed_t, att_t, partner(send), *gains),
            (shape((replicas, chunk_rows + (0 if layer else 32), width), BF),),
        )
        if layer:
            upstream = tie(upstream, attn_chunks)
        own_grads[layer] = own_rows(upstream)
    acts = jnp.stack(to_owner(own_out[0], own_out[1]))
    grads = jnp.stack(to_owner(own_grads[0], own_grads[1]))
    half = ff_cols // 2
    pieces = lax.all_to_all(attn_chunks, "replica", 0, 0, tiled=True)
    last = jnp.sum(pieces.astype(F32), axis=0)
    ffn_one, mixed = reduced
    ffn_lo, ffn_hi = to_owner(mixed[:, : 3 * half], ffn_one)
    attn_lo, attn_hi = to_owner(last[:chunk_rows, :wide].astype(BF), mixed[:, 3 * half :])
    lines = last[chunk_rows : chunk_rows + 24]
    values = jnp.concatenate([lines[:8], lines[8:16], lines[16:]], axis=1)[:, :d_model]
    values = values[:4] + values[4:]
    gain_parts = to_owner(values[:2], values[2:])
    gains_total = gain_parts[0] + gain_parts[1]

    def halves(start):
        return jnp.concatenate(
            [ffn_lo[:, start : start + half], ffn_hi[:, start : start + half]], axis=1
        ).astype(F32)

    final_gate, final_up = halves(0), halves(half)
    final_down = halves(2 * half).T
    final_q, final_k = attn_lo[:, :q_cols].astype(F32), attn_lo[:, q_cols:].astype(F32)
    final_out, final_v = attn_hi[:, :o_cols].astype(F32), attn_hi[:, o_cols:].astype(F32)
    return (
        acts[None],
        grads[None],
        final_q[None],
        final_k[None],
        final_v[None],
        final_out[None],
        final_gate[None],
        final_up[None],
        final_down[None],
        gains_total[None],
    )


def solution(mesh):
    placed = (
        P("replica", "shard", None),
        P("replica", "shard", None),
        P("replica", None),
        P("section", None, "shard"),
        P("section", None, "shard"),
        P("section", None, "shard"),
        P("section", None, "shard"),
        P("section", None, "shard"),
        P("section", None, "shard"),
        P("section", "shard", None),
        P("section", None, None),
    )
    return jax.shard_map(
        local,
        mesh=mesh,
        in_specs=placed,
        out_specs=(
            P("section", "replica", "shard", None),
            P("section", "replica", "shard", None),
            P("section", "replica", "shard"),
            P("section", "replica", "shard"),
            P("section", "replica", "shard"),
            P("section", "replica", "shard"),
            P("section", "replica", "shard"),
            P("section", "replica", "shard"),
            P("section", "shard", "replica"),
            P("section", None, None),
        ),
        check_vma=False,
    )
```

```python
import functools

import jax
import jax.numpy as jnp
from jax import lax
from jax.experimental import pallas as pl
from jax.experimental.pallas import tpu as pltpu
from jax.sharding import PartitionSpec as P

HQ = 15
KV = 5
HD = 64
GROUP = HQ // KV

epsilon = 1e-05
rope_base = 10000.0
masked_score = -1e30
scale = HD**-0.5
spare = 16

BF = jnp.bfloat16
F32 = jnp.float32


def dot(left, right, left_dim, right_dim):
    return lax.dot_general(
        left, right, (((left_dim,), (right_dim,)), ((), ())), preferred_element_type=F32
    )


def shape(dims, dtype):
    return jax.ShapeDtypeStruct(dims, dtype)


def call(body, name, arrays, outs, scratch=(), in_hbm=()):
    specs = [pl.BlockSpec(memory_space=pltpu.SMEM)] + [
        pl.BlockSpec(memory_space=pl.ANY if at in in_hbm else pltpu.VMEM)
        for at in range(1, len(arrays))
    ]
    return pl.pallas_call(
        body,
        name=name,
        in_specs=specs,
        out_specs=[pl.BlockSpec(memory_space=pltpu.VMEM) for _ in outs],
        out_shape=list(outs),
        scratch_shapes=list(scratch),
        compiler_params=pltpu.CompilerParams(vmem_limit_bytes=60 * 1024 * 1024),
    )(*arrays)


class Copies:
    def __init__(self, sems):
        self.sems, self.plain, self.cond = sems, [], []
        self.used = 0

    def _make(self, source, target):
        sem = self.sems.at[self.used]
        self.used += 1
        return pltpu.make_async_copy(source, target, sem)

    def add(self, source, target):
        copy = self._make(source, target)
        copy.start()
        self.plain.append(copy)

    def add_when(self, cond, pairs):
        made = [self._make(source, target) for source, target in pairs]

        @pl.when(cond)
        def _():
            for copy in made:
                copy.start()

        self.cond.append((cond, made))

    def wait(self):
        for copy in self.plain:
            copy.wait()
        for cond, made in self.cond:

            @pl.when(cond)
            def _(made=made):
                for copy in made:
                    copy.wait()


def start_pieces(place, sources, pieces, sems):
    core, shard_at = place[0], place[1]
    own, one, two, half, half_other = sources
    low, total = half.shape[0], own.shape[0]
    copies = Copies(sems)

    def rows(block, source, first, last, source_first):
        out = []
        for start, size, target, base in pieces:
            lo, hi = max(start, first), min(start + size, last)
            if lo < hi:
                at = pl.multiple_of(base + block * size + (lo - start), 16)
                out.append(
                    (
                        source.at[pl.ds(lo - source_first, hi - lo)],
                        target.at[pl.ds(at, hi - lo)],
                    )
                )
        return out

    for block, source in (
        (shard_at, own),
        (shard_at ^ (1 + core), one),
        (shard_at ^ (2 - core), two),
    ):
        for pair in rows(block, source, 0, total, 0):
            copies.add(*pair)
    across = shard_at ^ 3
    for at in range(2):
        top, bottom = (half, half_other) if at == 0 else (half_other, half)
        copies.add_when(
            core == at,
            rows(across, top, 0, low, 0) + rows(across, bottom, low, total, total - low),
        )
    return copies


def start_qkv(place, sources, target, sems, widths):
    q_cols, kv_cols, _ = widths
    pieces = (
        (0, q_cols, target, 0),
        (q_cols, kv_cols, target, 4 * q_cols),
        (q_cols + kv_cols, kv_cols, target, 4 * (q_cols + kv_cols)),
    )
    return start_pieces(place, sources, pieces, sems)


def start_out(place, sources, target, sems, widths):
    q_cols, kv_cols, o_cols = widths
    first = q_cols + 2 * kv_cols
    return start_pieces(place, sources, ((first, o_cols, target, 0),), sems)


def start_ffn(place, layer, sources, targets, sems):
    copies = Copies(sems)
    for (own, other), target in zip(sources, targets):
        copies.add_when(place[0] == layer, [(own, target)])
        copies.add_when(place[0] != layer, [(other, target)])
    return copies


def turn_rows(values, cosine, sine_table, heads):
    half = HD // 2
    out = []
    for head in range(heads):
        a = values[head * HD : head * HD + half]
        b = values[head * HD + half : (head + 1) * HD]
        out.append(a * cosine - b * sine_table)
        out.append(b * cosine + a * sine_table)
    return jnp.concatenate(out, axis=0)


def allowed_rows(seg_col, seg_row):
    length = seg_col.shape[0]
    key_at = lax.broadcasted_iota(jnp.int32, (length, length), 0)
    query_at = lax.broadcasted_iota(jnp.int32, (length, length), 1)
    return (seg_col == seg_row) & (key_at <= query_at)


def inverse_rms(values):
    return lax.rsqrt(jnp.mean(values * values, axis=-1, keepdims=True) + epsilon)


def place_rows(place, sources, target):
    for at, source in enumerate(sources):
        rows = source.shape[0]
        target[pl.ds(pl.multiple_of((place[1] ^ at) * rows, 16), rows)] = source[...]


def forward_body(layer, widths, place, *refs):
    refs = list(refs)

    def take(count):
        out = refs[:count]
        del refs[:count]
        return out

    if layer:
        before, a, a_in, b, b_in = take(5)
    else:
        x_sources = take(4)
    attn_sources = take(5)
    ffn_sources = [take(2) for _ in range(3)]
    gain, cosine_ref, sine_ref, seg_col, seg_row = take(5)
    x_out, normed_t, q_t, k_t, v_t, lse, att_t = take(7)
    middle_out, normed_f_out, gate_out, up_out, hidden_out = take(5)
    parts = take(1 if layer else 2)
    w_qkv, w_out, w_gate, w_up, w_down, qkv_sems, out_sems, ffn_sems = take(8)
    qkv_copies = start_qkv(place, attn_sources, w_qkv, qkv_sems, widths)
    out_copies = start_out(place, attn_sources, w_out, out_sems, widths)
    ffn_copies = start_ffn(place, layer, ffn_sources, (w_gate, w_up, w_down), ffn_sems)
    if layer:
        half = a.shape[0]
        x_out[:half] = (before[:half] + (a[...].astype(F32) + a_in[...].astype(F32))).astype(BF)
        x_out[half:] = (before[half:] + (b[...].astype(F32) + b_in[...].astype(F32))).astype(BF)
    else:
        place_rows(place, x_sources, x_out)
    x = x_out[...].astype(F32)
    normed = (x * inverse_rms(x) * gain[0:1]).astype(BF)
    normed_t[...] = normed.T
    cosine, sine_table = cosine_ref[...], sine_ref[...]
    allowed = allowed_rows(seg_col[...], seg_row[...])
    qkv_copies.wait()
    q_rows, kv_rows = HQ * HD, KV * HD
    qkv = dot(w_qkv[...], normed, 1, 1)
    q_t[...] = turn_rows(qkv[:q_rows], cosine, sine_table, HQ).astype(BF)
    k_t[...] = turn_rows(qkv[q_rows : q_rows + kv_rows], cosine, sine_table, KV).astype(BF)
    v_t[...] = qkv[q_rows + kv_rows :].astype(BF)
    lse[...] = jnp.zeros(lse.shape, F32)
    for head in range(HQ):
        key = (head // GROUP) * HD
        scores = dot(k_t[key : key + HD], q_t[head * HD : (head + 1) * HD], 0, 0) * scale
        scores = jnp.where(allowed, scores, masked_score)
        top = jnp.max(scores, axis=0, keepdims=True)
        weight = jnp.exp(scores - top)
        total = jnp.sum(weight, axis=0, keepdims=True)
        lse[head : head + 1] = top + jnp.log(total)
        probs = (weight * (1.0 / total)).astype(BF)
        att_t[head * HD : (head + 1) * HD] = dot(v_t[key : key + HD], probs, 1, 0).astype(BF)
    attended = att_t[...].T
    out_copies.wait()
    middle = x + dot(attended, w_out[...], 1, 1)
    middle_out[...] = middle
    normed_f = (middle * inverse_rms(middle) * gain[1:2]).astype(BF)
    normed_f_out[...] = normed_f
    ffn_copies.wait()
    gate_pre = dot(normed_f, w_gate[...], 1, 0)
    up_pre = dot(normed_f, w_up[...], 1, 0)
    gate_out[...] = gate_pre
    up_out[...] = up_pre
    hidden = (gate_pre / (1.0 + jnp.exp(-gate_pre)) * up_pre).astype(BF)
    hidden_out[...] = hidden
    part = dot(hidden, w_down[...], 1, 1).astype(BF)
    if layer:
        parts[0][...] = part
    else:
        half = part.shape[0] // 2
        parts[0][...] = part[:half]
        parts[1][...] = part[half:]


def ffn_backward_body(layer, place, *refs):
    refs = list(refs)

    def take(count):
        out = refs[:count]
        del refs[:count]
        return out

    up_sources = take(4 if layer else 1)
    gate_ref, up_ref, hidden_ref, normed_ref = take(4)
    sources = [take(2) for _ in range(3)]
    send, keep, part_a, part_b = take(4)
    if layer:
        (upstream_ref,) = take(1)
        place_rows(place, up_sources, upstream_ref)
    else:
        (upstream_ref,) = up_sources
    w_gate, w_up, w_down, sems = take(4)
    copies = start_ffn(place, layer, sources, (w_gate, w_up, w_down), sems)
    upstream, gate_pre, up_pre = upstream_ref[...], gate_ref[...], up_ref[...]
    length = upstream.shape[0]
    send[length : 2 * length] = normed_ref[...]
    send[2 * length : 3 * length] = upstream
    send[3 * length :] = jnp.zeros((spare, upstream.shape[1]), BF)
    copies.wait()
    d_hidden = dot(upstream, w_down[...], 1, 0)
    sigma = 1.0 / (1.0 + jnp.exp(-gate_pre))
    d_gate = (d_hidden * up_pre * sigma * (1.0 + gate_pre * (1.0 - sigma))).astype(BF)
    d_up = (d_hidden * gate_pre * sigma).astype(BF)
    part = (dot(d_gate, w_gate[...], 1, 1) + dot(d_up, w_up[...], 1, 1)).astype(BF)
    half = part.shape[0] // 2
    part_a[...] = part[:half]
    part_b[...] = part[half:]
    wide = d_gate.shape[1] // 2
    blocks = (d_gate, d_up, hidden_ref[...])
    low = jnp.concatenate([block[:, :wide] for block in blocks], axis=1)
    high = jnp.concatenate([block[:, wide:] for block in blocks], axis=1)
    is_low = place[0] == 0

    @pl.when(is_low)
    def _():
        keep[...] = low
        send[:length] = high

    @pl.when(jnp.logical_not(is_low))
    def _():
        keep[...] = high
        send[:length] = low


def ffn_grad_body(place, keep, normed, upstream, got, *rest):
    *rider, out = rest
    chunks, rows, _ = out.shape
    wide = keep.shape[1]
    two_thirds = wide * 2 // 3
    length = keep.shape[0]
    got_normed, got_up = got[length : 2 * length], got[2 * length : 3 * length]
    first = dot(normed[...], keep[:, :two_thirds], 0, 0) + dot(
        got_normed, got[:length, :two_thirds], 0, 0
    )
    second = dot(upstream[...], keep[:, two_thirds:], 0, 0) + dot(
        got_up, got[:length, two_thirds:], 0, 0
    )
    both = jnp.concatenate([first, second], axis=1).astype(BF)
    if rider:
        out[:, :, wide:] = rider[0][...]
    for chunk in range(chunks):
        out[chunk, :, :wide] = both[chunk * rows : (chunk + 1) * rows]


def attention_backward_body(widths, place, *refs):
    refs = list(refs)

    def take(count):
        out = refs[:count]
        del refs[:count]
        return out

    q_cols, kv_cols, o_cols = widths
    a, a_in, b, b_in, upstream_ref, middle_ref, x_ref = take(7)
    normed_t, q_t, k_t, v_t, lse, att_t = take(6)
    attn_sources = take(5)
    gain, cosine_ref, sine_ref, seg_col, seg_row = take(5)
    d_in, send, keep, gain_out = take(4)
    w_qkv, w_out, d_rows, d_norm_f, qkv_sems, out_sems = take(6)
    out_copies = start_out(place, attn_sources, w_out, out_sems, widths)
    qkv_copies = start_qkv(place, attn_sources, w_qkv, qkv_sems, widths)

    half = a.shape[0]
    d_norm_f[:half] = a[...].astype(F32) + a_in[...].astype(F32)
    d_norm_f[half:] = b[...].astype(F32) + b_in[...].astype(F32)
    middle = middle_ref[...]
    inv_f = inverse_rms(middle)
    d_normed_f = d_norm_f[...]
    gain_out[1:2] = jnp.sum(d_normed_f * middle * inv_f, axis=0, keepdims=True)
    scaled = d_normed_f * gain[1:2]
    d_middle = (
        upstream_ref[...].astype(F32)
        + inv_f * scaled
        - middle * (inv_f * inv_f * inv_f) * jnp.mean(scaled * middle, axis=-1, keepdims=True)
    )
    d_middle_b = d_middle.astype(BF)
    cosine, sine_table = cosine_ref[...], -sine_ref[...]
    allowed = allowed_rows(seg_col[...], seg_row[...])
    out_copies.wait()
    d_att = dot(d_middle_b, w_out[...], 1, 0).astype(BF).T
    q_rows, kv_rows = HQ * HD, KV * HD
    for kv in range(KV):
        key = kv * HD
        keys, values = k_t[key : key + HD], v_t[key : key + HD]
        d_keys = d_values = None
        for head in range(kv * GROUP, (kv + 1) * GROUP):
            at = head * HD
            queries = q_t[at : at + HD]
            scores = dot(keys, queries, 0, 0) * scale
            scores = jnp.where(allowed, scores, masked_score)
            probs = jnp.exp(scores - lse[head : head + 1])
            d_out = d_att[at : at + HD]
            delta = jnp.sum(
                d_out.astype(F32) * att_t[at : at + HD].astype(F32), axis=0, keepdims=True
            )
            d_probs = dot(values, d_out, 0, 0)
            d_scores = (probs * (d_probs - delta) * scale).astype(BF)
            d_queries = dot(keys, d_scores, 1, 0)
            d_rows[at : at + HD] = turn_rows(d_queries, cosine, sine_table, 1).astype(BF)
            key_part = dot(queries, d_scores, 1, 1)
            value_part = dot(d_out, probs.astype(BF), 1, 1)
            d_keys = key_part if d_keys is None else d_keys + key_part
            d_values = value_part if d_values is None else d_values + value_part
        at = q_rows + key
        d_rows[at : at + HD] = turn_rows(d_keys, cosine, sine_table, 1).astype(BF)
        d_rows[at + kv_rows : at + kv_rows + HD] = d_values.astype(BF)
    qkv_copies.wait()
    d_normed = dot(d_rows[...].T, w_qkv[...], 1, 0)
    x = x_ref[...].astype(F32)
    inv = inverse_rms(x)
    gain_out[0:1] = jnp.sum(d_normed * x * inv, axis=0, keepdims=True)
    scaled = d_normed * gain[0:1]
    d_in[...] = (
        d_middle
        + inv * scaled
        - x * (inv * inv * inv) * jnp.mean(scaled * x, axis=-1, keepdims=True)
    ).astype(BF)

    core, shard_at = place[0], place[1]
    rows_d = d_middle_b.shape[1]
    choose = (
        lax.broadcasted_iota(jnp.int32, (o_cols, rows_d), 1)
        == lax.broadcasted_iota(jnp.int32, (o_cols, rows_d), 0) + shard_at * o_cols
    )
    own_out = dot(jnp.where(choose, 1.0, 0.0).astype(BF), d_middle_b, 1, 1).astype(BF)
    own_q = d_rows[pl.ds(pl.multiple_of(shard_at * q_cols, 16), q_cols)]
    own_k = d_rows[pl.ds(pl.multiple_of(q_rows + shard_at * kv_cols, 16), kv_cols)]
    own_v = d_rows[pl.ds(pl.multiple_of(q_rows + kv_rows + shard_at * kv_cols, 16), kv_cols)]
    wide = normed_t.shape[0]
    send[:wide] = normed_t[...]
    last = 2 * wide

    @pl.when(core == 0)
    def _():
        keep[:q_cols] = own_q
        keep[q_cols:] = own_k
        send[wide:last] = att_t[...]
        send[last : last + o_cols] = own_out
        send[last + o_cols :] = own_v

    @pl.when(core != 0)
    def _():
        keep[:o_cols] = own_out
        keep[o_cols:] = own_v
        send[wide:last] = normed_t[...]
        send[last : last + q_cols] = own_q
        send[last + q_cols :] = own_k


def attention_grad_body(place, keep, normed_t, att_t, got, *rest):
    *gains, out = rest
    chunks, all_rows, width = out.shape
    rows = normed_t.shape[0] // chunks
    d_model = normed_t.shape[0]
    wide = keep.shape[0]
    cols = wide * 3 // 4
    second = dot(normed_t[...], keep[cols:], 1, 1) + dot(
        got[:d_model], got[2 * d_model + cols :], 1, 1
    )
    second = second.astype(BF)
    theirs = dot(got[d_model : 2 * d_model], got[2 * d_model : 2 * d_model + cols], 1, 1)

    if gains:
        out[:, :, wide:] = jnp.zeros((chunks, all_rows, width - wide), BF)
        values = jnp.concatenate([part[...] for part in gains], axis=0)
        high = values.astype(BF).astype(F32)
        both = jnp.concatenate([high, values - high], axis=0)
        both = jnp.concatenate([both, jnp.zeros((both.shape[0], 3 * width - d_model), F32)], axis=1)
        lines = [both[:, at * width : (at + 1) * width] for at in range(3)]
        lines.append(jnp.zeros((all_rows - rows - 3 * both.shape[0], width), F32))
        block = jnp.concatenate(lines, axis=0).astype(BF)
        for chunk in range(chunks):
            out[chunk, rows:] = block

    def finish(mine):
        first = (dot(mine[...], keep[:cols], 1, 1) + theirs).astype(BF)
        for chunk in range(chunks):
            out[chunk, :rows, :cols] = first[chunk * rows : (chunk + 1) * rows]
            out[chunk, :rows, cols:wide] = second[chunk * rows : (chunk + 1) * rows]

    @pl.when(place[0] == 0)
    def _():
        finish(normed_t)

    @pl.when(place[0] != 0)
    def _():
        finish(att_t)


def turn_body(layer, flips, place, *refs):
    out = refs[-1]

    def fill(which):
        at = 0
        for index, flip in enumerate(flips):
            weight = refs[2 * index + which]
            if flip:
                cols = weight.shape[1]
                same = lax.broadcasted_iota(jnp.int32, (cols, cols), 0) == (
                    lax.broadcasted_iota(jnp.int32, (cols, cols), 1)
                )
                block = dot(jnp.where(same, 1.0, 0.0).astype(BF), weight[...], 1, 1).astype(BF)
            else:
                block = weight[...]
            out[at : at + block.shape[0]] = block
            at += block.shape[0]
        out[at:] = jnp.zeros((out.shape[0] - at, out.shape[1]), BF)

    @pl.when(place[0] == layer)
    def _():
        fill(0)

    @pl.when(place[0] != layer)
    def _():
        fill(1)


def after(value, before):
    return pl.pallas_call(
        lambda value, before, out: None,
        name="after",
        in_specs=[pl.BlockSpec(memory_space=pl.ANY)] * 2,
        out_specs=pl.BlockSpec(memory_space=pl.ANY),
        out_shape=shape(value.shape, value.dtype),
        input_output_aliases={0: 0},
    )(value, before)


def tie(value, *before):
    return lax.optimization_barrier((value, *before))[0]


def swap(block, axis, bit):
    return lax.ppermute(block, axis, [(i, i ^ bit) for i in range(lax.axis_size(axis))])


def swap_chips(block, other=False):
    bits = (2, 1) if other else (1, 2)
    return lax.ppermute(
        block,
        ("section", "shard"),
        [(core * 4 + at, core * 4 + (at ^ bits[core])) for core in range(2) for at in range(4)],
    )


def rope_tables(segments):
    length = segments.shape[-1]
    position = jnp.arange(length, dtype=jnp.int32)
    before = jnp.concatenate([segments[:1] - 1, segments[:-1]])
    starts = jnp.where(segments != before, position, 0)
    starts = jnp.max(
        jnp.where(position[None, :] <= position[:, None], starts[None, :], 0), axis=1
    )
    places = (position - starts).astype(F32)
    frequency = rope_base ** (jnp.arange(HD // 2, dtype=F32) * (-2.0 / HD))
    angles = frequency[:, None] * places[None, :]
    return (jnp.cos(angles), jnp.sin(angles))


def local(
    inputs,
    cotangent,
    segments,
    attn_q,
    attn_k,
    attn_v,
    attn_out,
    ffn_gate,
    ffn_up,
    ffn_down,
    norm_gains,
):
    core = lax.axis_index("section")
    shard_at = lax.axis_index("shard")
    place = jnp.stack([core, shard_at]).astype(jnp.int32)
    first = core == 0
    block_len, d_model = inputs.shape[1:]
    replicas = lax.axis_size("replica")
    q_cols, kv_cols, o_cols = attn_q.shape[2], attn_k.shape[2], attn_out.shape[2]
    ff_cols = ffn_gate.shape[2]
    widths = (q_cols, kv_cols, o_cols)
    q_rows, kv_rows = 4 * q_cols, 4 * kv_cols

    def partner(block):
        return swap(block, "section", 1)

    def pick(zero, one):
        return jnp.where(first, zero, one)

    def mine(stacked):
        return lax.dynamic_index_in_dim(stacked, core, 0, keepdims=False)

    length = 4 * block_len

    def gathered_rows(own):
        return [own] + [swap(own, "shard", bit) for bit in (1, 2, 3)]

    def turned(layer, weights, flips):
        rows = sum(own.shape[1 if flip else 0] for (own, _), flip in zip(weights, flips))
        (out,) = call(
            functools.partial(turn_body, layer, flips),
            "turn",
            (place, *[array for pair in weights for array in pair]),
            (shape((rows + spare, d_model), BF),),
        )
        return out

    def start_gather(own, one, before=(), last=()):
        low = (own.shape[0] // 2 + 15) // 16 * 16
        sent = lax.dynamic_slice_in_dim(one, core * (own.shape[0] - low), low, 0)
        half = swap_chips(tie(sent, *before) if before else sent, other=True)
        two = partner(one)
        return [own, one, two, half, partner(tie(half, *last) if last else half)]

    seg = mine(segments)
    tables = rope_tables(seg) + (seg[:, None], seg[None, :])

    gain_other = partner(norm_gains[0])
    gain_layers = [pick(norm_gains[0], gain_other), pick(gain_other, norm_gains[0])]
    x_sources = gathered_rows(mine(inputs))
    pairs = [(own, partner(own)) for own in (attn_q[0], attn_k[0].T, attn_v[0].T, attn_out[0])]
    flips = (True, False, False, True)
    rows0 = turned(0, pairs, flips)
    rows1 = turned(1, [(tie(own, rows0), other) for own, other in pairs], flips)
    ffn_other = [partner(tie(own, rows0)) for own in (ffn_gate[0], ffn_up[0], ffn_down[0].T)]
    one0, rows1, *settled = lax.optimization_barrier(
        (swap_chips(tie(rows0, *x_sources[1:])), rows1, *ffn_other, *tables, *gain_layers)
    )
    ffn_other, tables, gain_layers = settled[:3], tuple(settled[3:7]), settled[7:]
    attn0 = start_gather(rows0, one0)
    ffn_sources = []
    for own, other in zip((ffn_gate[0], ffn_up[0], ffn_down[0].T), ffn_other):
        ffn_sources += [own, other]
    one1 = swap_chips(tie(rows1, attn0[3]))

    attn_scratch = (
        pltpu.VMEM((q_rows + 2 * kv_rows, d_model), BF),
        pltpu.VMEM((4 * o_cols, d_model), BF),
    )
    ffn_scratch = (
        pltpu.VMEM((d_model, ff_cols), BF),
        pltpu.VMEM((d_model, ff_cols), BF),
        pltpu.VMEM((d_model, ff_cols), BF),
    )
    qkv_sems = pltpu.SemaphoreType.DMA((20,))
    out_sems = pltpu.SemaphoreType.DMA((8,))
    ffn_sems = pltpu.SemaphoreType.DMA((6,))
    half_rows = shape((length // 2, d_model), BF)

    def forward(layer, entry):
        parts = [shape((length, d_model), BF)] if layer else [half_rows, half_rows]
        start = 1 + len(entry)
        return call(
            functools.partial(forward_body, layer, widths),
            "forward",
            (place, *entry, *attn_layers[layer], *ffn_sources, gain_layers[layer], *tables),
            [
                shape((length, d_model), BF),
                shape((d_model, length), BF),
                shape((q_rows, length), BF),
                shape((kv_rows, length), BF),
                shape((kv_rows, length), BF),
                shape((16, length), F32),
                shape((q_rows, length), BF),
                shape((length, d_model), F32),
                shape((length, d_model), BF),
                shape((length, ff_cols), F32),
                shape((length, ff_cols), F32),
                shape((length, ff_cols), BF),
            ]
            + parts,
            attn_scratch + ffn_scratch + (qkv_sems, out_sems, ffn_sems),
            range(start, start + 11),
        )

    def exchange(a, b):
        a_in, b_in = swap(a, "shard", 1), swap(b, "shard", 2)
        a = (a.astype(F32) + a_in.astype(F32)).astype(BF)
        b = (b.astype(F32) + b_in.astype(F32)).astype(BF)
        return (a, swap(a, "shard", 2), b, swap(b, "shard", 1)), a_in

    def own_rows(full):
        return lax.dynamic_slice_in_dim(full, shard_at * block_len, block_len, 0)

    attn_layers = [attn0, None]
    x0, *saved0, part_a, part_b = forward(0, x_sources)
    summed, received = exchange(part_a, part_b)
    attn_layers[1] = start_gather(rows1, tie(one1, part_a), (received,), (summed[1], summed[3]))
    cot_sources = gathered_rows(tie(mine(cotangent), attn_layers[1][3]))
    x1, *saved1, part = forward(1, (saved0[6], *summed))
    xs, saved = (x0, x1), (saved0, saved1)

    side, low = shard_at // 2, shard_at % 2
    two_blocks = 2 * block_len
    near = lax.dynamic_slice_in_dim(part, side * two_blocks, two_blocks, 0)
    far = lax.dynamic_slice_in_dim(part, (1 - side) * two_blocks, two_blocks, 0)
    near = near.astype(F32) + swap(far, "shard", 2).astype(F32)
    mine_block = lax.dynamic_slice_in_dim(near, low * block_len, block_len, 0)
    sent = lax.dynamic_slice_in_dim(near, (1 - low) * block_len, block_len, 0).astype(BF)
    total = mine_block + swap(sent, "shard", 1).astype(F32)
    own_out = [own_rows(x1), (own_rows(saved1[6]) + total).astype(BF)]

    def to_owner(zero, one):
        got = partner(pick(one, zero))
        return pick(zero, got), pick(got, one)

    own_grads, gains_out = [None, None], [None, None]
    reduced = []
    chunk_rows = d_model // replicas

    def reduce(chunks):
        return lax.psum_scatter(chunks, "replica", scatter_dimension=0, tiled=False)

    for layer in (1, 0):
        (normed_t, q_t, k_t, v_t, lse, att_t, middle, normed_f, gate_pre, up_pre, hidden) = saved[layer]
        entry = cot_sources if layer else [upstream]
        half_ff = 3 * (ff_cols // 2)
        send, keep, part_a, part_b, *assembled = call(
            functools.partial(ffn_backward_body, layer),
            "ffn_backward",
            (place, *entry, gate_pre, up_pre, hidden, normed_f, *ffn_sources),
            [
                shape((3 * length + spare, d_model), BF),
                shape((length, half_ff), BF),
                half_rows,
                half_rows,
            ]
            + ([shape((length, d_model), BF)] if layer else []),
            ffn_scratch + (ffn_sems,),
            range(5 + len(entry), 11 + len(entry)),
        )
        if layer:
            (upstream,) = assembled
        sums, _ = exchange(part_a, part_b)
        got = partner(send)
        rider = () if layer else (attn_chunks,)
        (ffn_chunks,) = call(
            ffn_grad_body,
            "ffn_grad",
            (place, keep, normed_f, upstream, got, *rider),
            (shape((replicas, chunk_rows, half_ff + (0 if layer else o_cols + kv_cols)), BF),),
        )
        if layer:
            reduced.append(reduce(ffn_chunks))
        else:
            ffn_chunks = after(ffn_chunks, reduced[0])
            reduced.append(reduce(ffn_chunks))
        sums = [tie(sums[0], ffn_chunks), *sums[1:]]
        wide = o_cols + kv_cols
        upstream, send, keep, gains_out[layer] = call(
            functools.partial(attention_backward_body, widths),
            "attention_backward",
            (place, *sums, upstream, middle, xs[layer], normed_t, q_t, k_t, v_t, lse, att_t)
            + (*attn_layers[layer], gain_layers[layer])
            + tables,
            (
                shape((length, d_model), BF),
                shape((2 * d_model + wide, length), BF),
                shape((wide, length), BF),
                shape((2, d_model), F32),
            ),
            attn_scratch
            + (
                pltpu.VMEM((q_rows + 2 * kv_rows, length), BF),
                pltpu.VMEM((length, d_model), F32),
                qkv_sems,
                out_sems,
            ),
            range(14, 19),
        )
        width = wide if layer else (wide + 127) // 128 * 128
        gains = () if layer else tuple(gains_out)
        (attn_chunks,) = call(
            attention_grad_body,
            "attention_grad",
            (place, keep, normed_t, att_t, partner(send), *gains),
            (shape((replicas, chunk_rows + (0 if layer else 32), width), BF),),
        )
        if layer:
            upstream = tie(upstream, attn_chunks)
        own_grads[layer] = own_rows(upstream)
    acts = jnp.stack(to_owner(own_out[0], own_out[1]))
    grads = jnp.stack(to_owner(own_grads[0], own_grads[1]))
    half = ff_cols // 2
    ffn_one, mixed = reduced
    ffn_lo, ffn_hi = to_owner(mixed[:, : 3 * half], ffn_one)

    def halves(start):
        return jnp.concatenate(
            [ffn_lo[:, start : start + half], ffn_hi[:, start : start + half]], axis=1
        ).astype(F32)

    final_gate, final_up = halves(0), halves(half)
    final_down = halves(2 * half).T
    pieces = lax.all_to_all(attn_chunks, "replica", 0, 0, tiled=True)
    last = jnp.sum(pieces.astype(F32), axis=0)
    attn_lo, attn_hi = to_owner(last[:chunk_rows, :wide].astype(BF), mixed[:, 3 * half :])
    lines = last[chunk_rows : chunk_rows + 24]
    values = jnp.concatenate([lines[:8], lines[8:16], lines[16:]], axis=1)[:, :d_model]
    values = values[:4] + values[4:]
    gain_parts = to_owner(values[:2], values[2:])
    gains_total = gain_parts[0] + gain_parts[1]
    final_q, final_k = attn_lo[:, :q_cols].astype(F32), attn_lo[:, q_cols:].astype(F32)
    final_out, final_v = attn_hi[:, :o_cols].astype(F32), attn_hi[:, o_cols:].astype(F32)
    return (
        acts[None],
        grads[None],
        final_q[None],
        final_k[None],
        final_v[None],
        final_out[None],
        final_gate[None],
        final_up[None],
        final_down[None],
        gains_total[None],
    )


def solution(mesh):
    placed = (
        P("replica", "shard", None),
        P("replica", "shard", None),
        P("replica", None),
        P("section", None, "shard"),
        P("section", None, "shard"),
        P("section", None, "shard"),
        P("section", None, "shard"),
        P("section", None, "shard"),
        P("section", None, "shard"),
        P("section", "shard", None),
        P("section", None, None),
    )
    return jax.shard_map(
        local,
        mesh=mesh,
        in_specs=placed,
        out_specs=(
            P("section", "replica", "shard", None),
            P("section", "replica", "shard", None),
            P("section", "replica", "shard"),
            P("section", "replica", "shard"),
            P("section", "replica", "shard"),
            P("section", "replica", "shard"),
            P("section", "replica", "shard"),
            P("section", "replica", "shard"),
            P("section", "shard", "replica"),
            P("section", None, None),
        ),
        check_vma=False,
    )
```

```python
import functools

import jax
import jax.numpy as jnp
from jax import lax
from jax.experimental import pallas as pl
from jax.experimental.pallas import tpu as pltpu
from jax.sharding import PartitionSpec as P

HQ = 15
KV = 5
HD = 64
GROUP = HQ // KV

epsilon = 1e-05
rope_base = 10000.0
masked_score = -1e30
scale = HD**-0.5
spare = 16

BF = jnp.bfloat16
F32 = jnp.float32


def dot(left, right, left_dim, right_dim):
    return lax.dot_general(
        left, right, (((left_dim,), (right_dim,)), ((), ())), preferred_element_type=F32
    )


def shape(dims, dtype):
    return jax.ShapeDtypeStruct(dims, dtype)


def call(body, name, arrays, outs, scratch=(), in_hbm=()):
    specs = [pl.BlockSpec(memory_space=pltpu.SMEM)] + [
        pl.BlockSpec(memory_space=pl.ANY if at in in_hbm else pltpu.VMEM)
        for at in range(1, len(arrays))
    ]
    return pl.pallas_call(
        body,
        name=name,
        in_specs=specs,
        out_specs=[pl.BlockSpec(memory_space=pltpu.VMEM) for _ in outs],
        out_shape=list(outs),
        scratch_shapes=list(scratch),
        compiler_params=pltpu.CompilerParams(vmem_limit_bytes=60 * 1024 * 1024),
    )(*arrays)


class Copies:
    def __init__(self, sems):
        self.sems, self.plain, self.cond = sems, [], []
        self.used = 0

    def _make(self, source, target):
        sem = self.sems.at[self.used]
        self.used += 1
        return pltpu.make_async_copy(source, target, sem)

    def add(self, source, target):
        copy = self._make(source, target)
        copy.start()
        self.plain.append(copy)

    def add_when(self, cond, pairs):
        made = [self._make(source, target) for source, target in pairs]

        @pl.when(cond)
        def _():
            for copy in made:
                copy.start()

        self.cond.append((cond, made))

    def wait(self):
        for copy in self.plain:
            copy.wait()
        for cond, made in self.cond:

            @pl.when(cond)
            def _(made=made):
                for copy in made:
                    copy.wait()


def start_pieces(place, sources, pieces, sems):
    core, shard_at = place[0], place[1]
    own, one, two, half, half_other = sources
    low, total = half.shape[0], own.shape[0]
    copies = Copies(sems)

    def rows(block, source, first, last, source_first):
        out = []
        for start, size, target, base in pieces:
            lo, hi = max(start, first), min(start + size, last)
            if lo < hi:
                at = pl.multiple_of(base + block * size + (lo - start), 16)
                out.append(
                    (
                        source.at[pl.ds(lo - source_first, hi - lo)],
                        target.at[pl.ds(at, hi - lo)],
                    )
                )
        return out

    for block, source in (
        (shard_at, own),
        (shard_at ^ (1 + core), one),
        (shard_at ^ (2 - core), two),
    ):
        for pair in rows(block, source, 0, total, 0):
            copies.add(*pair)
    across = shard_at ^ 3
    for at in range(2):
        top, bottom = (half, half_other) if at == 0 else (half_other, half)
        copies.add_when(
            core == at,
            rows(across, top, 0, low, 0) + rows(across, bottom, low, total, total - low),
        )
    return copies


def start_qkv(place, sources, target, sems, widths):
    q_cols, kv_cols = widths[:2]
    pieces = (
        (0, q_cols, target, 0),
        (q_cols, kv_cols, target, 4 * q_cols),
        (q_cols + kv_cols, kv_cols, target, 4 * (q_cols + kv_cols)),
    )
    return start_pieces(place, sources, pieces, sems)


def start_out(place, sources, target, sems, widths):
    _, _, o_cols, first = widths
    return start_pieces(place, sources, ((first, o_cols, target, 0),), sems)


def start_ffn(place, layer, sources, targets, sems):
    copies = Copies(sems)
    for (own, other), target in zip(sources, targets):
        copies.add_when(place[0] == layer, [(own, target)])
        copies.add_when(place[0] != layer, [(other, target)])
    return copies


def turn_rows(values, cosine, sine_table, heads):
    half = HD // 2
    out = []
    for head in range(heads):
        a = values[head * HD : head * HD + half]
        b = values[head * HD + half : (head + 1) * HD]
        out.append(a * cosine - b * sine_table)
        out.append(b * cosine + a * sine_table)
    return jnp.concatenate(out, axis=0)


def allowed_rows(seg_col, seg_row):
    length = seg_col.shape[0]
    key_at = lax.broadcasted_iota(jnp.int32, (length, length), 0)
    query_at = lax.broadcasted_iota(jnp.int32, (length, length), 1)
    return (seg_col == seg_row) & (key_at <= query_at)


def inverse_rms(values):
    return lax.rsqrt(jnp.mean(values * values, axis=-1, keepdims=True) + epsilon)


def place_rows(place, sources, target):
    for at, source in enumerate(sources):
        rows = source.shape[0]
        target[pl.ds(pl.multiple_of((place[1] ^ at) * rows, 16), rows)] = source[...]


def project_body(place, *refs):
    x_sources, (rows, gain, x_out, normed_t, part) = refs[:4], refs[4:]
    place_rows(place, x_sources, x_out)
    x = x_out[...].astype(F32)
    normed = (x * inverse_rms(x) * gain[0:1]).astype(BF)
    normed_t[...] = normed.T
    part[...] = dot(rows[...], normed, 1, 1).astype(BF)


def forward_body(layer, widths, place, *refs):
    refs = list(refs)

    def take(count):
        out = refs[:count]
        del refs[:count]
        return out

    if layer:
        before, a, a_in, b, b_in = take(5)
        qkv_sources = take(5)
    else:
        (x_ref,) = take(1)
        qkv_parts = take(4)
    out_sources = take(5)
    ffn_sources = [take(2) for _ in range(3)]
    gain, cosine_ref, sine_ref, seg_col, seg_row = take(5)
    if layer:
        x_out, normed_t = take(2)
    q_t, k_t, v_t, lse, att_t = take(5)
    middle_out, normed_f_out, gate_out, up_out, hidden_out = take(5)
    parts = take(1 if layer else 2)
    w_qkv, w_out, w_gate, w_up, w_down, qkv_sems, out_sems, ffn_sems = take(8)
    if layer:
        qkv_copies = start_qkv(place, qkv_sources, w_qkv, qkv_sems, widths)
    out_copies = start_out(place, out_sources, w_out, out_sems, widths)
    ffn_copies = start_ffn(place, layer, ffn_sources, (w_gate, w_up, w_down), ffn_sems)
    if layer:
        half = a.shape[0]
        x_out[:half] = (before[:half] + (a[...].astype(F32) + a_in[...].astype(F32))).astype(BF)
        x_out[half:] = (before[half:] + (b[...].astype(F32) + b_in[...].astype(F32))).astype(BF)
        x = x_out[...].astype(F32)
        normed = (x * inverse_rms(x) * gain[0:1]).astype(BF)
        normed_t[...] = normed.T
        qkv_copies.wait()
        qkv = dot(w_qkv[...], normed, 1, 1)
    else:
        x = x_ref[...].astype(F32)
        q_cols, kv_cols = widths[:2]
        for at, part in enumerate(qkv_parts):
            block = place[1] ^ at
            for start, size in ((0, q_cols), (q_cols, kv_cols), (q_cols + kv_cols, kv_cols)):
                to = pl.multiple_of(4 * start + block * size, 16)
                w_qkv[pl.ds(to, size)] = part[start : start + size]
        qkv = w_qkv[...].astype(F32)
    cosine, sine_table = cosine_ref[...], sine_ref[...]
    allowed = allowed_rows(seg_col[...], seg_row[...])
    q_rows, kv_rows = HQ * HD, KV * HD
    q_t[...] = turn_rows(qkv[:q_rows], cosine, sine_table, HQ).astype(BF)
    k_t[...] = turn_rows(qkv[q_rows : q_rows + kv_rows], cosine, sine_table, KV).astype(BF)
    v_t[...] = qkv[q_rows + kv_rows :].astype(BF)
    lse[...] = jnp.zeros(lse.shape, F32)
    for head in range(HQ):
        key = (head // GROUP) * HD
        scores = dot(k_t[key : key + HD], q_t[head * HD : (head + 1) * HD], 0, 0) * scale
        scores = jnp.where(allowed, scores, masked_score)
        top = jnp.max(scores, axis=0, keepdims=True)
        weight = jnp.exp(scores - top)
        total = jnp.sum(weight, axis=0, keepdims=True)
        lse[head : head + 1] = top + jnp.log(total)
        probs = (weight * (1.0 / total)).astype(BF)
        att_t[head * HD : (head + 1) * HD] = dot(v_t[key : key + HD], probs, 1, 0).astype(BF)
    attended = att_t[...].T
    out_copies.wait()
    middle = x + dot(attended, w_out[...], 1, 1)
    middle_out[...] = middle
    normed_f = (middle * inverse_rms(middle) * gain[1:2]).astype(BF)
    normed_f_out[...] = normed_f
    ffn_copies.wait()
    gate_pre = dot(normed_f, w_gate[...], 1, 0)
    up_pre = dot(normed_f, w_up[...], 1, 0)
    gate_out[...] = gate_pre
    up_out[...] = up_pre
    hidden = (gate_pre / (1.0 + jnp.exp(-gate_pre)) * up_pre).astype(BF)
    hidden_out[...] = hidden
    part = dot(hidden, w_down[...], 1, 1).astype(BF)
    if layer:
        parts[0][...] = part
    else:
        half = part.shape[0] // 2
        parts[0][...] = part[:half]
        parts[1][...] = part[half:]


def ffn_backward_body(layer, place, *refs):
    refs = list(refs)

    def take(count):
        out = refs[:count]
        del refs[:count]
        return out

    up_sources = take(4 if layer else 1)
    gate_ref, up_ref, hidden_ref, normed_ref = take(4)
    sources = [take(2) for _ in range(3)]
    send, keep, part_a, part_b = take(4)
    if layer:
        (upstream_ref,) = take(1)
        place_rows(place, up_sources, upstream_ref)
    else:
        (upstream_ref,) = up_sources
    w_gate, w_up, w_down, sems = take(4)
    copies = start_ffn(place, layer, sources, (w_gate, w_up, w_down), sems)
    upstream, gate_pre, up_pre = upstream_ref[...], gate_ref[...], up_ref[...]
    length = upstream.shape[0]
    send[length : 2 * length] = normed_ref[...]
    send[2 * length : 3 * length] = upstream
    send[3 * length :] = jnp.zeros((spare, upstream.shape[1]), BF)
    copies.wait()
    d_hidden = dot(upstream, w_down[...], 1, 0)
    sigma = 1.0 / (1.0 + jnp.exp(-gate_pre))
    d_gate = (d_hidden * up_pre * sigma * (1.0 + gate_pre * (1.0 - sigma))).astype(BF)
    d_up = (d_hidden * gate_pre * sigma).astype(BF)
    part = (dot(d_gate, w_gate[...], 1, 1) + dot(d_up, w_up[...], 1, 1)).astype(BF)
    half = part.shape[0] // 2
    part_a[...] = part[:half]
    part_b[...] = part[half:]
    wide = d_gate.shape[1] // 2
    blocks = (d_gate, d_up, hidden_ref[...])
    low = jnp.concatenate([block[:, :wide] for block in blocks], axis=1)
    high = jnp.concatenate([block[:, wide:] for block in blocks], axis=1)
    is_low = place[0] == 0

    @pl.when(is_low)
    def _():
        keep[...] = low
        send[:length] = high

    @pl.when(jnp.logical_not(is_low))
    def _():
        keep[...] = high
        send[:length] = low


def ffn_grad_body(place, keep, normed, upstream, got, *rest):
    *rider, out = rest
    chunks, rows, _ = out.shape
    wide = keep.shape[1]
    two_thirds = wide * 2 // 3
    length = keep.shape[0]
    got_normed, got_up = got[length : 2 * length], got[2 * length : 3 * length]
    first = dot(normed[...], keep[:, :two_thirds], 0, 0) + dot(
        got_normed, got[:length, :two_thirds], 0, 0
    )
    second = dot(upstream[...], keep[:, two_thirds:], 0, 0) + dot(
        got_up, got[:length, two_thirds:], 0, 0
    )
    both = jnp.concatenate([first, second], axis=1).astype(BF)
    if rider:
        out[:, :, wide:] = rider[0][...]
    for chunk in range(chunks):
        out[chunk, :, :wide] = both[chunk * rows : (chunk + 1) * rows]


def attention_backward_body(widths, place, *refs):
    refs = list(refs)

    def take(count):
        out = refs[:count]
        del refs[:count]
        return out

    q_cols, kv_cols, o_cols = widths[:3]
    a, a_in, b, b_in, upstream_ref, middle_ref, x_ref = take(7)
    normed_t, q_t, k_t, v_t, lse, att_t = take(6)
    qkv_sources, out_sources = take(5), take(5)
    gain, cosine_ref, sine_ref, seg_col, seg_row = take(5)
    d_in, send, keep, gain_out = take(4)
    w_qkv, w_out, d_rows, d_norm_f, qkv_sems, out_sems = take(6)
    out_copies = start_out(place, out_sources, w_out, out_sems, widths)
    qkv_copies = start_qkv(place, qkv_sources, w_qkv, qkv_sems, widths)

    half = a.shape[0]
    d_norm_f[:half] = a[...].astype(F32) + a_in[...].astype(F32)
    d_norm_f[half:] = b[...].astype(F32) + b_in[...].astype(F32)
    middle = middle_ref[...]
    inv_f = inverse_rms(middle)
    d_normed_f = d_norm_f[...]
    gain_out[1:2] = jnp.sum(d_normed_f * middle * inv_f, axis=0, keepdims=True)
    scaled = d_normed_f * gain[1:2]
    d_middle = (
        upstream_ref[...].astype(F32)
        + inv_f * scaled
        - middle * (inv_f * inv_f * inv_f) * jnp.mean(scaled * middle, axis=-1, keepdims=True)
    )
    d_middle_b = d_middle.astype(BF)
    cosine, sine_table = cosine_ref[...], -sine_ref[...]
    allowed = allowed_rows(seg_col[...], seg_row[...])
    out_copies.wait()
    d_att = dot(d_middle_b, w_out[...], 1, 0).astype(BF).T
    q_rows, kv_rows = HQ * HD, KV * HD
    for kv in range(KV):
        key = kv * HD
        keys, values = k_t[key : key + HD], v_t[key : key + HD]
        d_keys = d_values = None
        for head in range(kv * GROUP, (kv + 1) * GROUP):
            at = head * HD
            queries = q_t[at : at + HD]
            scores = dot(keys, queries, 0, 0) * scale
            scores = jnp.where(allowed, scores, masked_score)
            probs = jnp.exp(scores - lse[head : head + 1])
            d_out = d_att[at : at + HD]
            delta = jnp.sum(
                d_out.astype(F32) * att_t[at : at + HD].astype(F32), axis=0, keepdims=True
            )
            d_probs = dot(values, d_out, 0, 0)
            d_scores = (probs * (d_probs - delta) * scale).astype(BF)
            d_queries = dot(keys, d_scores, 1, 0)
            d_rows[at : at + HD] = turn_rows(d_queries, cosine, sine_table, 1).astype(BF)
            key_part = dot(queries, d_scores, 1, 1)
            value_part = dot(d_out, probs.astype(BF), 1, 1)
            d_keys = key_part if d_keys is None else d_keys + key_part
            d_values = value_part if d_values is None else d_values + value_part
        at = q_rows + key
        d_rows[at : at + HD] = turn_rows(d_keys, cosine, sine_table, 1).astype(BF)
        d_rows[at + kv_rows : at + kv_rows + HD] = d_values.astype(BF)
    qkv_copies.wait()
    d_normed = dot(d_rows[...].T, w_qkv[...], 1, 0)
    x = x_ref[...].astype(F32)
    inv = inverse_rms(x)
    gain_out[0:1] = jnp.sum(d_normed * x * inv, axis=0, keepdims=True)
    scaled = d_normed * gain[0:1]
    d_in[...] = (
        d_middle
        + inv * scaled
        - x * (inv * inv * inv) * jnp.mean(scaled * x, axis=-1, keepdims=True)
    ).astype(BF)

    core, shard_at = place[0], place[1]
    rows_d = d_middle_b.shape[1]
    choose = (
        lax.broadcasted_iota(jnp.int32, (o_cols, rows_d), 1)
        == lax.broadcasted_iota(jnp.int32, (o_cols, rows_d), 0) + shard_at * o_cols
    )
    own_out = dot(jnp.where(choose, 1.0, 0.0).astype(BF), d_middle_b, 1, 1).astype(BF)
    own_q = d_rows[pl.ds(pl.multiple_of(shard_at * q_cols, 16), q_cols)]
    own_k = d_rows[pl.ds(pl.multiple_of(q_rows + shard_at * kv_cols, 16), kv_cols)]
    own_v = d_rows[pl.ds(pl.multiple_of(q_rows + kv_rows + shard_at * kv_cols, 16), kv_cols)]
    wide = normed_t.shape[0]
    send[:wide] = normed_t[...]
    last = 2 * wide

    @pl.when(core == 0)
    def _():
        keep[:q_cols] = own_q
        keep[q_cols:] = own_k
        send[wide:last] = att_t[...]
        send[last : last + o_cols] = own_out
        send[last + o_cols :] = own_v

    @pl.when(core != 0)
    def _():
        keep[:o_cols] = own_out
        keep[o_cols:] = own_v
        send[wide:last] = normed_t[...]
        send[last : last + q_cols] = own_q
        send[last + q_cols :] = own_k


def attention_grad_body(place, keep, normed_t, att_t, got, *rest):
    *gains, out = rest
    chunks, all_rows, width = out.shape
    rows = normed_t.shape[0] // chunks
    d_model = normed_t.shape[0]
    wide = keep.shape[0]
    cols = wide * 3 // 4
    second = dot(normed_t[...], keep[cols:], 1, 1) + dot(
        got[:d_model], got[2 * d_model + cols :], 1, 1
    )
    second = second.astype(BF)
    theirs = dot(got[d_model : 2 * d_model], got[2 * d_model : 2 * d_model + cols], 1, 1)

    if gains:
        out[:, :, wide:] = jnp.zeros((chunks, all_rows, width - wide), BF)
        values = jnp.concatenate([part[...] for part in gains], axis=0)
        high = values.astype(BF).astype(F32)
        both = jnp.concatenate([high, values - high], axis=0)
        both = jnp.concatenate([both, jnp.zeros((both.shape[0], 3 * width - d_model), F32)], axis=1)
        lines = [both[:, at * width : (at + 1) * width] for at in range(3)]
        lines.append(jnp.zeros((all_rows - rows - 3 * both.shape[0], width), F32))
        block = jnp.concatenate(lines, axis=0).astype(BF)
        for chunk in range(chunks):
            out[chunk, rows:] = block

    def finish(mine):
        first = (dot(mine[...], keep[:cols], 1, 1) + theirs).astype(BF)
        for chunk in range(chunks):
            out[chunk, :rows, :cols] = first[chunk * rows : (chunk + 1) * rows]
            out[chunk, :rows, cols:wide] = second[chunk * rows : (chunk + 1) * rows]

    @pl.when(place[0] == 0)
    def _():
        finish(normed_t)

    @pl.when(place[0] != 0)
    def _():
        finish(att_t)


def turn_body(layer, flips, place, *refs):
    out = refs[-1]

    def fill(which):
        at = 0
        for index, flip in enumerate(flips):
            weight = refs[2 * index + which]
            if flip:
                cols = weight.shape[1]
                same = lax.broadcasted_iota(jnp.int32, (cols, cols), 0) == (
                    lax.broadcasted_iota(jnp.int32, (cols, cols), 1)
                )
                block = dot(jnp.where(same, 1.0, 0.0).astype(BF), weight[...], 1, 1).astype(BF)
            else:
                block = weight[...]
            out[at : at + block.shape[0]] = block
            at += block.shape[0]
        if out.shape[0] > at:
            out[at:] = jnp.zeros((out.shape[0] - at, out.shape[1]), BF)

    @pl.when(place[0] == layer)
    def _():
        fill(0)

    @pl.when(place[0] != layer)
    def _():
        fill(1)


def after(value, before):
    return pl.pallas_call(
        lambda value, before, out: None,
        name="after",
        in_specs=[pl.BlockSpec(memory_space=pl.ANY)] * 2,
        out_specs=pl.BlockSpec(memory_space=pl.ANY),
        out_shape=shape(value.shape, value.dtype),
        input_output_aliases={0: 0},
    )(value, before)


def tie(value, *before):
    return lax.optimization_barrier((value, *before))[0]


def swap(block, axis, bit):
    return lax.ppermute(block, axis, [(i, i ^ bit) for i in range(lax.axis_size(axis))])


def swap_chips(block, other=False):
    bits = (2, 1) if other else (1, 2)
    return lax.ppermute(
        block,
        ("section", "shard"),
        [(core * 4 + at, core * 4 + (at ^ bits[core])) for core in range(2) for at in range(4)],
    )


def rope_tables(segments):
    length = segments.shape[-1]
    position = jnp.arange(length, dtype=jnp.int32)
    before = jnp.concatenate([segments[:1] - 1, segments[:-1]])
    starts = jnp.where(segments != before, position, 0)
    starts = jnp.max(
        jnp.where(position[None, :] <= position[:, None], starts[None, :], 0), axis=1
    )
    places = (position - starts).astype(F32)
    frequency = rope_base ** (jnp.arange(HD // 2, dtype=F32) * (-2.0 / HD))
    angles = frequency[:, None] * places[None, :]
    return (jnp.cos(angles), jnp.sin(angles))


def local(
    inputs,
    cotangent,
    segments,
    attn_q,
    attn_k,
    attn_v,
    attn_out,
    ffn_gate,
    ffn_up,
    ffn_down,
    norm_gains,
):
    core = lax.axis_index("section")
    shard_at = lax.axis_index("shard")
    place = jnp.stack([core, shard_at]).astype(jnp.int32)
    first = core == 0
    block_len, d_model = inputs.shape[1:]
    replicas = lax.axis_size("replica")
    q_cols, kv_cols, o_cols = attn_q.shape[2], attn_k.shape[2], attn_out.shape[2]
    ff_cols = ffn_gate.shape[2]
    first_out = q_cols + 2 * kv_cols
    widths = [(q_cols, kv_cols, o_cols, first) for first in (0, first_out)]
    q_rows, kv_rows = 4 * q_cols, 4 * kv_cols

    def partner(block):
        return swap(block, "section", 1)

    def pick(zero, one):
        return jnp.where(first, zero, one)

    def mine(stacked):
        return lax.dynamic_index_in_dim(stacked, core, 0, keepdims=False)

    length = 4 * block_len

    def gathered_rows(own):
        return [own] + [swap(own, "shard", bit) for bit in (1, 2, 3)]

    def turned(layer, weights, flips):
        rows = sum(own.shape[1 if flip else 0] for (own, _), flip in zip(weights, flips))
        (out,) = call(
            functools.partial(turn_body, layer, flips),
            "turn",
            (place, *[array for pair in weights for array in pair]),
            (shape((rows + (0 if rows % 128 else spare), d_model), BF),),
        )
        return out

    def start_gather(own, one, before=(), last=()):
        low = (own.shape[0] // 2 + 15) // 16 * 16
        sent = lax.dynamic_slice_in_dim(one, core * (own.shape[0] - low), low, 0)
        half = swap_chips(tie(sent, *before) if before else sent, other=True)
        two = partner(one)
        return [own, one, two, half, partner(tie(half, *last) if last else half)]

    gain_other = partner(norm_gains[0])
    gain_layers = [pick(norm_gains[0], gain_other), pick(gain_other, norm_gains[0])]
    x_sources = gathered_rows(mine(inputs))
    pairs = [(own, partner(own)) for own in (attn_q[0], attn_k[0].T, attn_v[0].T, attn_out[0])]
    flips = (True, False, False, True)
    rows0 = turned(0, pairs[:3], flips[:3])
    seg = mine(tie(segments, rows0))
    tables = rope_tables(seg) + (seg[:, None], seg[None, :])
    x0, normed_t0, part0 = call(
        project_body,
        "project",
        (place, *x_sources, rows0, gain_layers[0]),
        (
            shape((length, d_model), BF),
            shape((d_model, length), BF),
            shape((rows0.shape[0], length), BF),
        ),
    )
    out0 = turned(0, [(tie(pairs[3][0], rows0), pairs[3][1])], flips[3:])
    out_one = swap_chips(out0)
    ffn_other = [partner(tie(own, rows0)) for own in (ffn_gate[0], ffn_up[0], ffn_down[0].T)]
    qkv_parts = gathered_rows(part0)
    out_layers = [start_gather(out0, out_one, (qkv_parts[1],)), None]
    rows1 = turned(1, [(tie(own, part0), other) for own, other in pairs], flips)
    *qkv_parts, rows1, a_, b_, c_, d_ = lax.optimization_barrier((*qkv_parts, rows1, *tables))
    tables = (a_, b_, c_, d_)
    ffn_sources = []
    for own, other in zip((ffn_gate[0], ffn_up[0], ffn_down[0].T), ffn_other):
        ffn_sources += [own, other]
    one1 = swap_chips(tie(rows1, qkv_parts[3], out_layers[0][3]))

    attn_scratch = (
        pltpu.VMEM((q_rows + 2 * kv_rows, d_model), BF),
        pltpu.VMEM((4 * o_cols, d_model), BF),
    )
    ffn_scratch = (
        pltpu.VMEM((d_model, ff_cols), BF),
        pltpu.VMEM((d_model, ff_cols), BF),
        pltpu.VMEM((d_model, ff_cols), BF),
    )
    qkv_sems = pltpu.SemaphoreType.DMA((20,))
    out_sems = pltpu.SemaphoreType.DMA((8,))
    ffn_sems = pltpu.SemaphoreType.DMA((6,))
    half_rows = shape((length // 2, d_model), BF)

    def forward(layer, entry):
        parts = [shape((length, d_model), BF)] if layer else [half_rows, half_rows]
        start = 1 + len(entry) - (5 if layer else 0)
        heads = [shape((length, d_model), BF), shape((d_model, length), BF)] if layer else []
        held = attn_scratch[0] if layer else pltpu.VMEM((q_rows + 2 * kv_rows, length), BF)
        return call(
            functools.partial(forward_body, layer, widths[layer]),
            "forward",
            (place, *entry, *out_layers[layer], *ffn_sources, gain_layers[layer], *tables),
            heads
            + [
                shape((q_rows, length), BF),
                shape((kv_rows, length), BF),
                shape((kv_rows, length), BF),
                shape((16, length), F32),
                shape((q_rows, length), BF),
                shape((length, d_model), F32),
                shape((length, d_model), BF),
                shape((length, ff_cols), F32),
                shape((length, ff_cols), F32),
                shape((length, ff_cols), BF),
            ]
            + parts,
            (held, attn_scratch[1]) + ffn_scratch + (qkv_sems, out_sems, ffn_sems),
            range(start, start + (16 if layer else 11)),
        )

    def exchange(a, b):
        a_in, b_in = swap(a, "shard", 1), swap(b, "shard", 2)
        a = (a.astype(F32) + a_in.astype(F32)).astype(BF)
        b = (b.astype(F32) + b_in.astype(F32)).astype(BF)
        return (a, swap(a, "shard", 2), b, swap(b, "shard", 1)), (a_in, b_in)

    def own_rows(full):
        return lax.dynamic_slice_in_dim(full, shard_at * block_len, block_len, 0)

    *saved0, part_a, part_b = forward(0, (x0, *qkv_parts))
    saved0 = [normed_t0] + saved0
    summed, received = exchange(part_a, part_b)
    out_layers[1] = start_gather(
        rows1, tie(one1, part_a), received, (summed[1], summed[3])
    )
    qkv_layers = [None, out_layers[1]]
    cot_sources = gathered_rows(tie(mine(cotangent), out_layers[1][3]))
    rows0_one = swap_chips(tie(rows0, out_layers[1][3]))
    x1, *saved1, part = forward(1, (saved0[6], *summed, *qkv_layers[1]))
    cot_sources[3] = tie(cot_sources[3], rows0_one)
    xs, saved = (x0, x1), (saved0, saved1)

    side, low = shard_at // 2, shard_at % 2
    two_blocks = 2 * block_len
    near = lax.dynamic_slice_in_dim(part, side * two_blocks, two_blocks, 0)
    far = lax.dynamic_slice_in_dim(part, (1 - side) * two_blocks, two_blocks, 0)
    near = near.astype(F32) + swap(far, "shard", 2).astype(F32)
    mine_block = lax.dynamic_slice_in_dim(near, low * block_len, block_len, 0)
    sent = lax.dynamic_slice_in_dim(near, (1 - low) * block_len, block_len, 0).astype(BF)
    total = mine_block + swap(sent, "shard", 1).astype(F32)
    own_out = [own_rows(x1), (own_rows(saved1[6]) + total).astype(BF)]

    def to_owner(zero, one):
        got = partner(pick(one, zero))
        return pick(zero, got), pick(got, one)

    own_grads, gains_out = [None, None], [None, None]
    reduced = []
    chunk_rows = d_model // replicas

    def reduce(chunks):
        return lax.psum_scatter(chunks, "replica", scatter_dimension=0, tiled=False)

    for layer in (1, 0):
        (normed_t, q_t, k_t, v_t, lse, att_t, middle, normed_f, gate_pre, up_pre, hidden) = saved[layer]
        entry = cot_sources if layer else [upstream]
        half_ff = 3 * (ff_cols // 2)
        send, keep, part_a, part_b, *assembled = call(
            functools.partial(ffn_backward_body, layer),
            "ffn_backward",
            (place, *entry, gate_pre, up_pre, hidden, normed_f, *ffn_sources),
            [
                shape((3 * length + spare, d_model), BF),
                shape((length, half_ff), BF),
                half_rows,
                half_rows,
            ]
            + ([shape((length, d_model), BF)] if layer else []),
            ffn_scratch + (ffn_sems,),
            range(5 + len(entry), 11 + len(entry)),
        )
        if layer:
            (upstream,) = assembled
        sums, _ = exchange(part_a, part_b)
        if layer:
            qkv_layers[0] = start_gather(rows0, tie(rows0_one, sums[3]))
        got = partner(send)
        rider = () if layer else (attn_chunks,)
        (ffn_chunks,) = call(
            ffn_grad_body,
            "ffn_grad",
            (place, keep, normed_f, upstream, got, *rider),
            (shape((replicas, chunk_rows, half_ff + (0 if layer else o_cols + kv_cols)), BF),),
        )
        if layer:
            reduced.append(reduce(ffn_chunks))
        else:
            ffn_chunks = after(ffn_chunks, reduced[0])
            reduced.append(reduce(ffn_chunks))
        sums = [tie(sums[0], ffn_chunks), *sums[1:]]
        wide = o_cols + kv_cols
        upstream, send, keep, gains_out[layer] = call(
            functools.partial(attention_backward_body, widths[layer]),
            "attention_backward",
            (place, *sums, upstream, middle, xs[layer], normed_t, q_t, k_t, v_t, lse, att_t)
            + (*qkv_layers[layer], *out_layers[layer], gain_layers[layer])
            + tables,
            (
                shape((length, d_model), BF),
                shape((2 * d_model + wide, length), BF),
                shape((wide, length), BF),
                shape((2, d_model), F32),
            ),
            attn_scratch
            + (
                pltpu.VMEM((q_rows + 2 * kv_rows, length), BF),
                pltpu.VMEM((length, d_model), F32),
                qkv_sems,
                out_sems,
            ),
            range(14, 24),
        )
        width = wide if layer else (wide + 127) // 128 * 128
        gains = () if layer else tuple(gains_out)
        (attn_chunks,) = call(
            attention_grad_body,
            "attention_grad",
            (place, keep, normed_t, att_t, partner(send), *gains),
            (shape((replicas, chunk_rows + (0 if layer else 32), width), BF),),
        )
        own_grads[layer] = own_rows(upstream)
        if layer:
            upstream = tie(upstream, attn_chunks, qkv_layers[0][3])
    acts = jnp.stack(to_owner(own_out[0], own_out[1]))
    grads = jnp.stack(to_owner(own_grads[0], own_grads[1]))
    half = ff_cols // 2
    ffn_one, mixed = reduced
    ffn_lo, ffn_hi = to_owner(mixed[:, : 3 * half], ffn_one)

    def halves(start):
        return jnp.concatenate(
            [ffn_lo[:, start : start + half], ffn_hi[:, start : start + half]], axis=1
        ).astype(F32)

    final_gate, final_up = halves(0), halves(half)
    final_down = halves(2 * half).T
    pieces = lax.all_to_all(attn_chunks, "replica", 0, 0, tiled=True)
    last = jnp.sum(pieces.astype(F32), axis=0)
    attn_lo, attn_hi = to_owner(last[:chunk_rows, :wide].astype(BF), mixed[:, 3 * half :])
    lines = last[chunk_rows : chunk_rows + 24]
    values = jnp.concatenate([lines[:8], lines[8:16], lines[16:]], axis=1)[:, :d_model]
    values = values[:4] + values[4:]
    gain_parts = to_owner(values[:2], values[2:])
    gains_total = gain_parts[0] + gain_parts[1]
    final_q, final_k = attn_lo[:, :q_cols].astype(F32), attn_lo[:, q_cols:].astype(F32)
    final_out, final_v = attn_hi[:, :o_cols].astype(F32), attn_hi[:, o_cols:].astype(F32)
    return (
        acts[None],
        grads[None],
        final_q[None],
        final_k[None],
        final_v[None],
        final_out[None],
        final_gate[None],
        final_up[None],
        final_down[None],
        gains_total[None],
    )


def solution(mesh):
    placed = (
        P("replica", "shard", None),
        P("replica", "shard", None),
        P("replica", None),
        P("section", None, "shard"),
        P("section", None, "shard"),
        P("section", None, "shard"),
        P("section", None, "shard"),
        P("section", None, "shard"),
        P("section", None, "shard"),
        P("section", "shard", None),
        P("section", None, None),
    )
    return jax.shard_map(
        local,
        mesh=mesh,
        in_specs=placed,
        out_specs=(
            P("section", "replica", "shard", None),
            P("section", "replica", "shard", None),
            P("section", "replica", "shard"),
            P("section", "replica", "shard"),
            P("section", "replica", "shard"),
            P("section", "replica", "shard"),
            P("section", "replica", "shard"),
            P("section", "replica", "shard"),
            P("section", "shard", "replica"),
            P("section", None, None),
        ),
        check_vma=False,
    )
```

```python
import functools

import jax
import jax.numpy as jnp
from jax import lax
from jax.experimental import pallas as pl
from jax.experimental.pallas import tpu as pltpu
from jax.sharding import PartitionSpec as P

HQ = 15
KV = 5
HD = 64
GROUP = HQ // KV

epsilon = 1e-05
rope_base = 10000.0
masked_score = -1e30
scale = HD**-0.5
spare = 16

BF = jnp.bfloat16
F32 = jnp.float32


def dot(left, right, left_dim, right_dim):
    return lax.dot_general(
        left, right, (((left_dim,), (right_dim,)), ((), ())), preferred_element_type=F32
    )


def shape(dims, dtype):
    return jax.ShapeDtypeStruct(dims, dtype)


def call(body, name, arrays, outs, scratch=(), in_hbm=()):
    specs = [pl.BlockSpec(memory_space=pltpu.SMEM)] + [
        pl.BlockSpec(memory_space=pl.ANY if at in in_hbm else pltpu.VMEM)
        for at in range(1, len(arrays))
    ]
    return pl.pallas_call(
        body,
        name=name,
        in_specs=specs,
        out_specs=[pl.BlockSpec(memory_space=pltpu.VMEM) for _ in outs],
        out_shape=list(outs),
        scratch_shapes=list(scratch),
        compiler_params=pltpu.CompilerParams(vmem_limit_bytes=60 * 1024 * 1024),
    )(*arrays)


class Copies:
    def __init__(self, sems):
        self.sems, self.plain, self.cond = sems, [], []
        self.used = 0

    def _make(self, source, target):
        sem = self.sems.at[self.used]
        self.used += 1
        return pltpu.make_async_copy(source, target, sem)

    def add(self, source, target):
        copy = self._make(source, target)
        copy.start()
        self.plain.append(copy)

    def add_when(self, cond, pairs):
        made = [self._make(source, target) for source, target in pairs]

        @pl.when(cond)
        def _():
            for copy in made:
                copy.start()

        self.cond.append((cond, made))

    def wait(self):
        for copy in self.plain:
            copy.wait()
        for cond, made in self.cond:

            @pl.when(cond)
            def _(made=made):
                for copy in made:
                    copy.wait()


def start_pieces(place, sources, pieces, sems):
    core, shard_at = place[0], place[1]
    own, one, two, half, half_other = sources
    low, total = half.shape[0], own.shape[0]
    copies = Copies(sems)

    def rows(block, source, first, last, source_first):
        out = []
        for start, size, target, base in pieces:
            lo, hi = max(start, first), min(start + size, last)
            if lo < hi:
                at = pl.multiple_of(base + block * size + (lo - start), 16)
                out.append(
                    (
                        source.at[pl.ds(lo - source_first, hi - lo)],
                        target.at[pl.ds(at, hi - lo)],
                    )
                )
        return out

    for block, source in (
        (shard_at, own),
        (shard_at ^ (1 + core), one),
        (shard_at ^ (2 - core), two),
    ):
        for pair in rows(block, source, 0, total, 0):
            copies.add(*pair)
    across = shard_at ^ 3
    for at in range(2):
        top, bottom = (half, half_other) if at == 0 else (half_other, half)
        copies.add_when(
            core == at,
            rows(across, top, 0, low, 0) + rows(across, bottom, low, total, total - low),
        )
    return copies


def start_qkv(place, sources, target, sems, widths):
    q_cols, kv_cols = widths[:2]
    pieces = (
        (0, q_cols, target, 0),
        (q_cols, kv_cols, target, 4 * q_cols),
        (q_cols + kv_cols, kv_cols, target, 4 * (q_cols + kv_cols)),
    )
    return start_pieces(place, sources, pieces, sems)


def start_out(place, sources, target, sems, widths):
    _, _, o_cols, first = widths
    return start_pieces(place, sources, ((first, o_cols, target, 0),), sems)


def start_ffn(place, layer, sources, targets, sems):
    copies = Copies(sems)
    for (own, other), target in zip(sources, targets):
        copies.add_when(place[0] == layer, [(own, target)])
        copies.add_when(place[0] != layer, [(other, target)])
    return copies


def turn_rows(values, cosine, sine_table, heads):
    half = HD // 2
    out = []
    for head in range(heads):
        a = values[head * HD : head * HD + half]
        b = values[head * HD + half : (head + 1) * HD]
        out.append(a * cosine - b * sine_table)
        out.append(b * cosine + a * sine_table)
    return jnp.concatenate(out, axis=0)


def allowed_rows(seg_col, seg_row):
    length = seg_col.shape[0]
    key_at = lax.broadcasted_iota(jnp.int32, (length, length), 0)
    query_at = lax.broadcasted_iota(jnp.int32, (length, length), 1)
    return (seg_col == seg_row) & (key_at <= query_at)


def inverse_rms(values):
    return lax.rsqrt(jnp.mean(values * values, axis=-1, keepdims=True) + epsilon)


def place_rows(place, sources, target):
    for at, source in enumerate(sources):
        rows = source.shape[0]
        target[pl.ds(pl.multiple_of((place[1] ^ at) * rows, 16), rows)] = source[...]


def project_body(place, *refs):
    x_sources, (rows, gain, x_out, normed_t, part) = refs[:4], refs[4:]
    place_rows(place, x_sources, x_out)
    x = x_out[...].astype(F32)
    normed = (x * inverse_rms(x) * gain[0:1]).astype(BF)
    normed_t[...] = normed.T
    part[...] = dot(rows[...], normed, 1, 1).astype(BF)


def forward_body(layer, widths, place, *refs):
    refs = list(refs)

    def take(count):
        out = refs[:count]
        del refs[:count]
        return out

    if layer:
        before, a, a_in, b, b_in = take(5)
        qkv_sources = take(5)
    else:
        (x_ref,) = take(1)
        qkv_parts = take(4)
    out_sources = take(5)
    ffn_sources = [take(2) for _ in range(3)]
    gain, cosine_ref, sine_ref, seg_col, seg_row = take(5)
    if layer:
        x_out, normed_t = take(2)
    q_t, k_t, v_t, lse, att_t = take(5)
    middle_out, normed_f_out, gate_out, up_out, hidden_out = take(5)
    parts = take(1 if layer else 2)
    w_qkv, w_out, w_gate, w_up, w_down, qkv_sems, out_sems, ffn_sems = take(8)
    if layer:
        qkv_copies = start_qkv(place, qkv_sources, w_qkv, qkv_sems, widths)
    out_copies = start_out(place, out_sources, w_out, out_sems, widths)
    ffn_copies = start_ffn(place, layer, ffn_sources, (w_gate, w_up, w_down), ffn_sems)
    if layer:
        half = a.shape[0]
        x_out[:half] = (before[:half] + (a[...].astype(F32) + a_in[...].astype(F32))).astype(BF)
        x_out[half:] = (before[half:] + (b[...].astype(F32) + b_in[...].astype(F32))).astype(BF)
        x = x_out[...].astype(F32)
        normed = (x * inverse_rms(x) * gain[0:1]).astype(BF)
        normed_t[...] = normed.T
        qkv_copies.wait()
        qkv = dot(w_qkv[...], normed, 1, 1)
    else:
        x = x_ref[...].astype(F32)
        q_cols, kv_cols = widths[:2]
        for at, part in enumerate(qkv_parts):
            block = place[1] ^ at
            for start, size in ((0, q_cols), (q_cols, kv_cols), (q_cols + kv_cols, kv_cols)):
                to = pl.multiple_of(4 * start + block * size, 16)
                w_qkv[pl.ds(to, size)] = part[start : start + size]
        qkv = w_qkv[...].astype(F32)
    cosine, sine_table = cosine_ref[...], sine_ref[...]
    allowed = allowed_rows(seg_col[...], seg_row[...])
    q_rows, kv_rows = HQ * HD, KV * HD
    q_t[...] = turn_rows(qkv[:q_rows], cosine, sine_table, HQ).astype(BF)
    k_t[...] = turn_rows(qkv[q_rows : q_rows + kv_rows], cosine, sine_table, KV).astype(BF)
    v_t[...] = qkv[q_rows + kv_rows :].astype(BF)
    lse[...] = jnp.zeros(lse.shape, F32)
    for head in range(HQ):
        key = (head // GROUP) * HD
        scores = dot(k_t[key : key + HD], q_t[head * HD : (head + 1) * HD], 0, 0) * scale
        scores = jnp.where(allowed, scores, masked_score)
        top = jnp.max(scores, axis=0, keepdims=True)
        weight = jnp.exp(scores - top)
        total = jnp.sum(weight, axis=0, keepdims=True)
        lse[head : head + 1] = top + jnp.log(total)
        probs = (weight * (1.0 / total)).astype(BF)
        att_t[head * HD : (head + 1) * HD] = dot(v_t[key : key + HD], probs, 1, 0).astype(BF)
    attended = att_t[...].T
    out_copies.wait()
    middle = x + dot(attended, w_out[...], 1, 1)
    middle_out[...] = middle
    normed_f = (middle * inverse_rms(middle) * gain[1:2]).astype(BF)
    normed_f_out[...] = normed_f
    ffn_copies.wait()
    gate_pre = dot(normed_f, w_gate[...], 1, 0)
    up_pre = dot(normed_f, w_up[...], 1, 0)
    gate_out[...] = gate_pre
    up_out[...] = up_pre
    hidden = (gate_pre / (1.0 + jnp.exp(-gate_pre)) * up_pre).astype(BF)
    hidden_out[...] = hidden
    part = dot(hidden, w_down[...], 1, 1).astype(BF)
    if layer:
        parts[0][...] = part
    else:
        half = part.shape[0] // 2
        parts[0][...] = part[:half]
        parts[1][...] = part[half:]


def ffn_backward_body(layer, place, *refs):
    refs = list(refs)

    def take(count):
        out = refs[:count]
        del refs[:count]
        return out

    up_sources = take(4 if layer else 1)
    gate_ref, up_ref, hidden_ref, normed_ref = take(4)
    sources = [take(2) for _ in range(3)]
    send, keep, part_a, part_b = take(4)
    if layer:
        (upstream_ref,) = take(1)
        place_rows(place, up_sources, upstream_ref)
    else:
        (upstream_ref,) = up_sources
    w_gate, w_up, w_down, sems = take(4)
    copies = start_ffn(place, layer, sources, (w_gate, w_up, w_down), sems)
    upstream, gate_pre, up_pre = upstream_ref[...], gate_ref[...], up_ref[...]
    length = upstream.shape[0]
    send[length : 2 * length] = normed_ref[...]
    send[2 * length : 3 * length] = upstream
    send[3 * length :] = jnp.zeros((spare, upstream.shape[1]), BF)
    copies.wait()
    d_hidden = dot(upstream, w_down[...], 1, 0)
    sigma = 1.0 / (1.0 + jnp.exp(-gate_pre))
    d_gate = (d_hidden * up_pre * sigma * (1.0 + gate_pre * (1.0 - sigma))).astype(BF)
    d_up = (d_hidden * gate_pre * sigma).astype(BF)
    part = (dot(d_gate, w_gate[...], 1, 1) + dot(d_up, w_up[...], 1, 1)).astype(BF)
    half = part.shape[0] // 2
    part_a[...] = part[:half]
    part_b[...] = part[half:]
    wide = d_gate.shape[1] // 2
    blocks = (d_gate, d_up, hidden_ref[...])
    low = jnp.concatenate([block[:, :wide] for block in blocks], axis=1)
    high = jnp.concatenate([block[:, wide:] for block in blocks], axis=1)
    is_low = place[0] == 0

    @pl.when(is_low)
    def _():
        keep[...] = low
        send[:length] = high

    @pl.when(jnp.logical_not(is_low))
    def _():
        keep[...] = high
        send[:length] = low


def ffn_grad_body(place, keep, normed, upstream, got, *rest):
    *rider, out = rest
    chunks, rows, _ = out.shape
    wide = keep.shape[1]
    two_thirds = wide * 2 // 3
    length = keep.shape[0]
    got_normed, got_up = got[length : 2 * length], got[2 * length : 3 * length]
    first = dot(normed[...], keep[:, :two_thirds], 0, 0) + dot(
        got_normed, got[:length, :two_thirds], 0, 0
    )
    second = dot(upstream[...], keep[:, two_thirds:], 0, 0) + dot(
        got_up, got[:length, two_thirds:], 0, 0
    )
    both = jnp.concatenate([first, second], axis=1).astype(BF)
    if rider:
        out[:, :, wide:] = rider[0][...]
    for chunk in range(chunks):
        out[chunk, :, :wide] = both[chunk * rows : (chunk + 1) * rows]


def attention_backward_body(widths, place, *refs):
    refs = list(refs)

    def take(count):
        out = refs[:count]
        del refs[:count]
        return out

    q_cols, kv_cols, o_cols = widths[:3]
    a, a_in, b, b_in, upstream_ref, middle_ref, x_ref = take(7)
    normed_t, q_t, k_t, v_t, lse, att_t = take(6)
    qkv_sources, out_sources = take(5), take(5)
    gain, cosine_ref, sine_ref, seg_col, seg_row = take(5)
    d_in, send, keep, gain_out = take(4)
    w_qkv, w_out, d_rows, d_norm_f, qkv_sems, out_sems = take(6)
    out_copies = start_out(place, out_sources, w_out, out_sems, widths)
    qkv_copies = start_qkv(place, qkv_sources, w_qkv, qkv_sems, widths)

    half = a.shape[0]
    d_norm_f[:half] = a[...].astype(F32) + a_in[...].astype(F32)
    d_norm_f[half:] = b[...].astype(F32) + b_in[...].astype(F32)
    middle = middle_ref[...]
    inv_f = inverse_rms(middle)
    d_normed_f = d_norm_f[...]
    gain_out[1:2] = jnp.sum(d_normed_f * middle * inv_f, axis=0, keepdims=True)
    scaled = d_normed_f * gain[1:2]
    d_middle = (
        upstream_ref[...].astype(F32)
        + inv_f * scaled
        - middle * (inv_f * inv_f * inv_f) * jnp.mean(scaled * middle, axis=-1, keepdims=True)
    )
    d_middle_b = d_middle.astype(BF)
    cosine, sine_table = cosine_ref[...], -sine_ref[...]
    allowed = allowed_rows(seg_col[...], seg_row[...])
    out_copies.wait()
    d_att = dot(d_middle_b, w_out[...], 1, 0).astype(BF).T
    q_rows, kv_rows = HQ * HD, KV * HD
    for kv in range(KV):
        key = kv * HD
        keys, values = k_t[key : key + HD], v_t[key : key + HD]
        d_keys = d_values = None
        for head in range(kv * GROUP, (kv + 1) * GROUP):
            at = head * HD
            queries = q_t[at : at + HD]
            scores = dot(keys, queries, 0, 0) * scale
            scores = jnp.where(allowed, scores, masked_score)
            probs = jnp.exp(scores - lse[head : head + 1])
            d_out = d_att[at : at + HD]
            delta = jnp.sum(
                d_out.astype(F32) * att_t[at : at + HD].astype(F32), axis=0, keepdims=True
            )
            d_probs = dot(values, d_out, 0, 0)
            d_scores = (probs * (d_probs - delta) * scale).astype(BF)
            d_queries = dot(keys, d_scores, 1, 0)
            d_rows[at : at + HD] = turn_rows(d_queries, cosine, sine_table, 1).astype(BF)
            key_part = dot(queries, d_scores, 1, 1)
            value_part = dot(d_out, probs.astype(BF), 1, 1)
            d_keys = key_part if d_keys is None else d_keys + key_part
            d_values = value_part if d_values is None else d_values + value_part
        at = q_rows + key
        d_rows[at : at + HD] = turn_rows(d_keys, cosine, sine_table, 1).astype(BF)
        d_rows[at + kv_rows : at + kv_rows + HD] = d_values.astype(BF)
    qkv_copies.wait()
    d_normed = dot(d_rows[...].T, w_qkv[...], 1, 0)
    x = x_ref[...].astype(F32)
    inv = inverse_rms(x)
    gain_out[0:1] = jnp.sum(d_normed * x * inv, axis=0, keepdims=True)
    scaled = d_normed * gain[0:1]
    d_in[...] = (
        d_middle
        + inv * scaled
        - x * (inv * inv * inv) * jnp.mean(scaled * x, axis=-1, keepdims=True)
    ).astype(BF)

    core, shard_at = place[0], place[1]
    rows_d = d_middle_b.shape[1]
    choose = (
        lax.broadcasted_iota(jnp.int32, (o_cols, rows_d), 1)
        == lax.broadcasted_iota(jnp.int32, (o_cols, rows_d), 0) + shard_at * o_cols
    )
    own_out = dot(jnp.where(choose, 1.0, 0.0).astype(BF), d_middle_b, 1, 1).astype(BF)
    own_q = d_rows[pl.ds(pl.multiple_of(shard_at * q_cols, 16), q_cols)]
    own_k = d_rows[pl.ds(pl.multiple_of(q_rows + shard_at * kv_cols, 16), kv_cols)]
    own_v = d_rows[pl.ds(pl.multiple_of(q_rows + kv_rows + shard_at * kv_cols, 16), kv_cols)]
    wide = normed_t.shape[0]
    send[:wide] = normed_t[...]
    last = 2 * wide

    @pl.when(core == 0)
    def _():
        keep[:q_cols] = own_q
        keep[q_cols:] = own_k
        send[wide:last] = att_t[...]
        send[last : last + o_cols] = own_out
        send[last + o_cols :] = own_v

    @pl.when(core != 0)
    def _():
        keep[:o_cols] = own_out
        keep[o_cols:] = own_v
        send[wide:last] = normed_t[...]
        send[last : last + q_cols] = own_q
        send[last + q_cols :] = own_k


def attention_grad_body(place, keep, normed_t, att_t, got, *rest):
    *gains, out = rest
    chunks, all_rows, width = out.shape
    rows = normed_t.shape[0] // chunks
    d_model = normed_t.shape[0]
    wide = keep.shape[0]
    cols = wide * 3 // 4
    second = dot(normed_t[...], keep[cols:], 1, 1) + dot(
        got[:d_model], got[2 * d_model + cols :], 1, 1
    )
    second = second.astype(BF)
    theirs = dot(got[d_model : 2 * d_model], got[2 * d_model : 2 * d_model + cols], 1, 1)

    if gains:
        out[:, :, wide:] = jnp.zeros((chunks, all_rows, width - wide), BF)
        values = jnp.concatenate([part[...] for part in gains], axis=0)
        high = values.astype(BF).astype(F32)
        both = jnp.concatenate([high, values - high], axis=0)
        both = jnp.concatenate([both, jnp.zeros((both.shape[0], 3 * width - d_model), F32)], axis=1)
        lines = [both[:, at * width : (at + 1) * width] for at in range(3)]
        lines.append(jnp.zeros((all_rows - rows - 3 * both.shape[0], width), F32))
        block = jnp.concatenate(lines, axis=0).astype(BF)
        for chunk in range(chunks):
            out[chunk, rows:] = block

    def finish(mine):
        first = (dot(mine[...], keep[:cols], 1, 1) + theirs).astype(BF)
        for chunk in range(chunks):
            out[chunk, :rows, :cols] = first[chunk * rows : (chunk + 1) * rows]
            out[chunk, :rows, cols:wide] = second[chunk * rows : (chunk + 1) * rows]

    @pl.when(place[0] == 0)
    def _():
        finish(normed_t)

    @pl.when(place[0] != 0)
    def _():
        finish(att_t)


def turn_body(layer, flips, place, *refs):
    out = refs[-1]

    def fill(which):
        at = 0
        for index, flip in enumerate(flips):
            weight = refs[2 * index + which]
            if flip:
                cols = weight.shape[1]
                same = lax.broadcasted_iota(jnp.int32, (cols, cols), 0) == (
                    lax.broadcasted_iota(jnp.int32, (cols, cols), 1)
                )
                block = dot(jnp.where(same, 1.0, 0.0).astype(BF), weight[...], 1, 1).astype(BF)
            else:
                block = weight[...]
            out[at : at + block.shape[0]] = block
            at += block.shape[0]
        if out.shape[0] > at:
            out[at:] = jnp.zeros((out.shape[0] - at, out.shape[1]), BF)

    @pl.when(place[0] == layer)
    def _():
        fill(0)

    @pl.when(place[0] != layer)
    def _():
        fill(1)


def after(value, before):
    return pl.pallas_call(
        lambda value, before, out: None,
        name="after",
        in_specs=[pl.BlockSpec(memory_space=pl.ANY)] * 2,
        out_specs=pl.BlockSpec(memory_space=pl.ANY),
        out_shape=shape(value.shape, value.dtype),
        input_output_aliases={0: 0},
    )(value, before)


def tie(value, *before):
    return lax.optimization_barrier((value, *before))[0]


def swap(block, axis, bit):
    return lax.ppermute(block, axis, [(i, i ^ bit) for i in range(lax.axis_size(axis))])


def swap_chips(block, other=False):
    bits = (2, 1) if other else (1, 2)
    return lax.ppermute(
        block,
        ("section", "shard"),
        [(core * 4 + at, core * 4 + (at ^ bits[core])) for core in range(2) for at in range(4)],
    )


def rope_tables(segments):
    length = segments.shape[-1]
    position = jnp.arange(length, dtype=jnp.int32)
    before = jnp.concatenate([segments[:1] - 1, segments[:-1]])
    starts = jnp.where(segments != before, position, 0)
    starts = jnp.max(
        jnp.where(position[None, :] <= position[:, None], starts[None, :], 0), axis=1
    )
    places = (position - starts).astype(F32)
    frequency = rope_base ** (jnp.arange(HD // 2, dtype=F32) * (-2.0 / HD))
    angles = frequency[:, None] * places[None, :]
    return (jnp.cos(angles), jnp.sin(angles))


def local(
    inputs,
    cotangent,
    segments,
    attn_q,
    attn_k,
    attn_v,
    attn_out,
    ffn_gate,
    ffn_up,
    ffn_down,
    norm_gains,
):
    core = lax.axis_index("section")
    shard_at = lax.axis_index("shard")
    place = jnp.stack([core, shard_at]).astype(jnp.int32)
    first = core == 0
    block_len, d_model = inputs.shape[1:]
    replicas = lax.axis_size("replica")
    q_cols, kv_cols, o_cols = attn_q.shape[2], attn_k.shape[2], attn_out.shape[2]
    ff_cols = ffn_gate.shape[2]
    first_out = q_cols + 2 * kv_cols
    widths = [(q_cols, kv_cols, o_cols, first) for first in (0, first_out)]
    q_rows, kv_rows = 4 * q_cols, 4 * kv_cols

    def partner(block):
        return swap(block, "section", 1)

    def pick(zero, one):
        return jnp.where(first, zero, one)

    def mine(stacked):
        return lax.dynamic_index_in_dim(stacked, core, 0, keepdims=False)

    length = 4 * block_len

    def gathered_rows(own):
        return [own] + [swap(own, "shard", bit) for bit in (1, 2, 3)]

    def turned(layer, weights, flips):
        rows = sum(own.shape[1 if flip else 0] for (own, _), flip in zip(weights, flips))
        (out,) = call(
            functools.partial(turn_body, layer, flips),
            "turn",
            (place, *[array for pair in weights for array in pair]),
            (shape((rows + (0 if rows % 128 else spare), d_model), BF),),
        )
        return out

    def start_gather(own, one, before=(), last=()):
        low = (own.shape[0] // 2 + 15) // 16 * 16
        sent = lax.dynamic_slice_in_dim(one, core * (own.shape[0] - low), low, 0)
        half = swap_chips(tie(sent, *before) if before else sent, other=True)
        two = partner(one)
        return [own, one, two, half, partner(tie(half, *last) if last else half)]

    gain_other = partner(norm_gains[0])
    gain_layers = [pick(norm_gains[0], gain_other), pick(gain_other, norm_gains[0])]
    x_sources = gathered_rows(mine(inputs))
    pairs = [(own, partner(own)) for own in (attn_q[0], attn_k[0].T, attn_v[0].T, attn_out[0])]
    flips = (True, False, False, True)
    rows0 = turned(0, pairs[:3], flips[:3])
    seg = mine(tie(segments, rows0))
    tables = rope_tables(seg) + (seg[:, None], seg[None, :])
    x0, normed_t0, part0 = call(
        project_body,
        "project",
        (place, *x_sources, rows0, gain_layers[0]),
        (
            shape((length, d_model), BF),
            shape((d_model, length), BF),
            shape((rows0.shape[0], length), BF),
        ),
    )
    out0 = turned(0, [(tie(pairs[3][0], rows0), pairs[3][1])], flips[3:])
    out_one = swap_chips(out0)
    ffn_other = [partner(tie(own, rows0)) for own in (ffn_gate[0], ffn_up[0], ffn_down[0].T)]
    qkv_parts = gathered_rows(part0)
    out_layers = [start_gather(out0, out_one, (qkv_parts[1],)), None]
    rows1 = turned(1, [(tie(own, part0), other) for own, other in pairs], flips)
    *qkv_parts, rows1, a_, b_, c_, d_ = lax.optimization_barrier((*qkv_parts, rows1, *tables))
    tables = (a_, b_, c_, d_)
    ffn_sources = []
    for own, other in zip((ffn_gate[0], ffn_up[0], ffn_down[0].T), ffn_other):
        ffn_sources += [own, other]
    one1 = swap_chips(tie(rows1, qkv_parts[3], out_layers[0][3]))

    attn_scratch = (
        pltpu.VMEM((q_rows + 2 * kv_rows, d_model), BF),
        pltpu.VMEM((4 * o_cols, d_model), BF),
    )
    ffn_scratch = (
        pltpu.VMEM((d_model, ff_cols), BF),
        pltpu.VMEM((d_model, ff_cols), BF),
        pltpu.VMEM((d_model, ff_cols), BF),
    )
    qkv_sems = pltpu.SemaphoreType.DMA((20,))
    out_sems = pltpu.SemaphoreType.DMA((8,))
    ffn_sems = pltpu.SemaphoreType.DMA((6,))
    half_rows = shape((length // 2, d_model), BF)

    def forward(layer, entry):
        parts = [shape((length, d_model), BF)] if layer else [half_rows, half_rows]
        start = 1 + len(entry) - (5 if layer else 0)
        heads = [shape((length, d_model), BF), shape((d_model, length), BF)] if layer else []
        held = attn_scratch[0] if layer else pltpu.VMEM((q_rows + 2 * kv_rows, length), BF)
        return call(
            functools.partial(forward_body, layer, widths[layer]),
            "forward",
            (place, *entry, *out_layers[layer], *ffn_sources, gain_layers[layer], *tables),
            heads
            + [
                shape((q_rows, length), BF),
                shape((kv_rows, length), BF),
                shape((kv_rows, length), BF),
                shape((16, length), F32),
                shape((q_rows, length), BF),
                shape((length, d_model), F32),
                shape((length, d_model), BF),
                shape((length, ff_cols), F32),
                shape((length, ff_cols), F32),
                shape((length, ff_cols), BF),
            ]
            + parts,
            (held, attn_scratch[1]) + ffn_scratch + (qkv_sems, out_sems, ffn_sems),
            range(start, start + (16 if layer else 11)),
        )

    def exchange(a, b):
        a_in, b_in = swap(a, "shard", 1), swap(b, "shard", 2)
        a = (a.astype(F32) + a_in.astype(F32)).astype(BF)
        b = (b.astype(F32) + b_in.astype(F32)).astype(BF)
        return (a, swap(a, "shard", 2), b, swap(b, "shard", 1)), (a_in, b_in)

    def own_rows(full):
        return lax.dynamic_slice_in_dim(full, shard_at * block_len, block_len, 0)

    *saved0, part_a, part_b = forward(0, (x0, *qkv_parts))
    saved0 = [normed_t0] + saved0
    summed, received = exchange(part_a, part_b)
    out_layers[1] = start_gather(
        rows1, tie(one1, part_a), received, (summed[1], summed[3])
    )
    qkv_layers = [None, out_layers[1]]
    cot_sources = gathered_rows(tie(mine(cotangent), out_layers[1][3]))
    rows0_one = swap_chips(tie(rows0, out_layers[1][3], summed[1], summed[3]))
    x1, *saved1, part = forward(1, (saved0[6], *summed, *qkv_layers[1]))
    cot_sources[3] = tie(cot_sources[3], rows0_one)
    xs, saved = (x0, x1), (saved0, saved1)

    side, low = shard_at // 2, shard_at % 2
    two_blocks = 2 * block_len
    near = lax.dynamic_slice_in_dim(part, side * two_blocks, two_blocks, 0)
    far = lax.dynamic_slice_in_dim(part, (1 - side) * two_blocks, two_blocks, 0)
    near = near.astype(F32) + swap(far, "shard", 2).astype(F32)
    mine_block = lax.dynamic_slice_in_dim(near, low * block_len, block_len, 0)
    sent = lax.dynamic_slice_in_dim(near, (1 - low) * block_len, block_len, 0).astype(BF)
    total = mine_block + swap(sent, "shard", 1).astype(F32)
    own_out = [own_rows(x1), (own_rows(saved1[6]) + total).astype(BF)]

    def to_owner(zero, one):
        got = partner(pick(one, zero))
        return pick(zero, got), pick(got, one)

    own_grads, gains_out = [None, None], [None, None]
    reduced = []
    chunk_rows = d_model // replicas

    def reduce(chunks):
        return lax.psum_scatter(chunks, "replica", scatter_dimension=0, tiled=False)

    for layer in (1, 0):
        (normed_t, q_t, k_t, v_t, lse, att_t, middle, normed_f, gate_pre, up_pre, hidden) = saved[layer]
        entry = cot_sources if layer else [upstream]
        half_ff = 3 * (ff_cols // 2)
        send, keep, part_a, part_b, *assembled = call(
            functools.partial(ffn_backward_body, layer),
            "ffn_backward",
            (place, *entry, gate_pre, up_pre, hidden, normed_f, *ffn_sources),
            [
                shape((3 * length + spare, d_model), BF),
                shape((length, half_ff), BF),
                half_rows,
                half_rows,
            ]
            + ([shape((length, d_model), BF)] if layer else []),
            ffn_scratch + (ffn_sems,),
            range(5 + len(entry), 11 + len(entry)),
        )
        if layer:
            (upstream,) = assembled
        sums, _ = exchange(part_a, part_b)
        if layer:
            qkv_layers[0] = start_gather(rows0, tie(rows0_one, sums[3]))
        got = partner(send)
        rider = () if layer else (attn_chunks,)
        (ffn_chunks,) = call(
            ffn_grad_body,
            "ffn_grad",
            (place, keep, normed_f, upstream, got, *rider),
            (shape((replicas, chunk_rows, half_ff + (0 if layer else o_cols + kv_cols)), BF),),
        )
        if layer:
            reduced.append(reduce(ffn_chunks))
        else:
            ffn_chunks = after(ffn_chunks, reduced[0])
            reduced.append(reduce(ffn_chunks))
        sums = [tie(sums[0], ffn_chunks), *sums[1:]]
        wide = o_cols + kv_cols
        upstream, send, keep, gains_out[layer] = call(
            functools.partial(attention_backward_body, widths[layer]),
            "attention_backward",
            (place, *sums, upstream, middle, xs[layer], normed_t, q_t, k_t, v_t, lse, att_t)
            + (*qkv_layers[layer], *out_layers[layer], gain_layers[layer])
            + tables,
            (
                shape((length, d_model), BF),
                shape((2 * d_model + wide, length), BF),
                shape((wide, length), BF),
                shape((2, d_model), F32),
            ),
            attn_scratch
            + (
                pltpu.VMEM((q_rows + 2 * kv_rows, length), BF),
                pltpu.VMEM((length, d_model), F32),
                qkv_sems,
                out_sems,
            ),
            range(14, 24),
        )
        width = wide if layer else (wide + 127) // 128 * 128
        gains = () if layer else tuple(gains_out)
        (attn_chunks,) = call(
            attention_grad_body,
            "attention_grad",
            (place, keep, normed_t, att_t, partner(send), *gains),
            (shape((replicas, chunk_rows + (0 if layer else 32), width), BF),),
        )
        own_grads[layer] = own_rows(upstream)
        if layer:
            upstream = tie(upstream, attn_chunks, qkv_layers[0][3])
    acts = jnp.stack(to_owner(own_out[0], own_out[1]))
    grads = jnp.stack(to_owner(own_grads[0], own_grads[1]))
    half = ff_cols // 2
    ffn_one, mixed = reduced
    ffn_lo, ffn_hi = to_owner(mixed[:, : 3 * half], ffn_one)

    def halves(start):
        return jnp.concatenate(
            [ffn_lo[:, start : start + half], ffn_hi[:, start : start + half]], axis=1
        ).astype(F32)

    final_gate, final_up = halves(0), halves(half)
    final_down = halves(2 * half).T
    pieces = lax.all_to_all(attn_chunks, "replica", 0, 0, tiled=True)
    last = jnp.sum(pieces.astype(F32), axis=0)
    attn_lo, attn_hi = to_owner(last[:chunk_rows, :wide].astype(BF), mixed[:, 3 * half :])
    lines = last[chunk_rows : chunk_rows + 24]
    values = jnp.concatenate([lines[:8], lines[8:16], lines[16:]], axis=1)[:, :d_model]
    values = values[:4] + values[4:]
    gain_parts = to_owner(values[:2], values[2:])
    gains_total = gain_parts[0] + gain_parts[1]
    final_q, final_k = attn_lo[:, :q_cols].astype(F32), attn_lo[:, q_cols:].astype(F32)
    final_out, final_v = attn_hi[:, :o_cols].astype(F32), attn_hi[:, o_cols:].astype(F32)
    return (
        acts[None],
        grads[None],
        final_q[None],
        final_k[None],
        final_v[None],
        final_out[None],
        final_gate[None],
        final_up[None],
        final_down[None],
        gains_total[None],
    )


def solution(mesh):
    placed = (
        P("replica", "shard", None),
        P("replica", "shard", None),
        P("replica", None),
        P("section", None, "shard"),
        P("section", None, "shard"),
        P("section", None, "shard"),
        P("section", None, "shard"),
        P("section", None, "shard"),
        P("section", None, "shard"),
        P("section", "shard", None),
        P("section", None, None),
    )
    return jax.shard_map(
        local,
        mesh=mesh,
        in_specs=placed,
        out_specs=(
            P("section", "replica", "shard", None),
            P("section", "replica", "shard", None),
            P("section", "replica", "shard"),
            P("section", "replica", "shard"),
            P("section", "replica", "shard"),
            P("section", "replica", "shard"),
            P("section", "replica", "shard"),
            P("section", "replica", "shard"),
            P("section", "shard", "replica"),
            P("section", None, None),
        ),
        check_vma=False,
    )
```
